32 devices in a mesh: grp: 2 (over y), req: 4 (over x, core), fsdp: 4 (over z).
Axes of the slice: x: 2, y: 2, z: 4, core: 2. Of those that a mesh axis runs over, the one named last changes fastest.
Arguments:
- hy_q: bfloat16 [8, 1024, 4096], P(('grp', 'req'), None, 'fsdp'), parts along dimension 0, may hold values from -6 to 6
- hy_k: bfloat16 [8, 1024, 4096], P(('grp', 'req'), None, 'fsdp'), parts along dimension 0, may hold values from -6 to 6
- hy_v: bfloat16 [8, 1024, 4096], P(('grp', 'req'), None, 'fsdp'), parts along dimension 0, may hold values from -6 to 6
- filter_taps: bfloat16 [4096, 128], P('fsdp', 'req'), may hold values from -0.8984375 to 0.8984375
- filter_decay: float32 [4096], P('fsdp'), may hold values from 0.003 to 0.08
- hy_cache: bfloat16 [32, 128, 4096], P(('grp', 'req'), None, 'fsdp'), parts along dimension 0, may hold values from -6 to 6
- at_q: bfloat16 [8, 1024, 4096], P(('grp', 'req'), None, 'fsdp'), parts along dimension 0, may hold values from -12 to 12, as said below
- at_k: bfloat16 [8, 1024, 4096], P(('grp', 'req'), None, 'fsdp'), parts along dimension 0, may hold values from -6 to 6
- at_v: bfloat16 [8, 1024, 4096], P(('grp', 'req'), None, 'fsdp'), parts along dimension 0, may hold values from -6 to 6
- kv_cache: bfloat16 [32, 2, 128, 4096], P(('grp', 'req'), None, None, 'fsdp'), parts along dimension 0, may hold values from -6 to 6, as said below
- prefix_owner: int32 [8, 8], P('grp'), parts along dimension 0, may hold values from 0 to 3, as said below
- prefix_slot: int32 [8, 8], P('grp'), parts along dimension 0, may hold values from 0 to 3, as said below
- prefix_count: int32 [8], P('grp'), parts along dimension 0, may hold values from 1 to 8, as said below
- new_length: int32 [8], P(('grp', 'req')), parts along dimension 0, may hold values from 1 to 1024, as said below
Outputs:
- hy_out: bfloat16 [8, 1024, 4096], P(('grp', 'req'), None, 'fsdp'), parts along dimension 0
- at_out: bfloat16 [8, 1024, 4096], P(('grp', 'req'), None, 'fsdp'), parts along dimension 0
The draws below stay inside these ranges and needn't reach their ends.
There are 2 independent parts, one for each index of `grp`. The reference program is written for one: setup_inputs(seed, part) draws one part's arguments, and reference() takes and returns one part's arrays. A program takes and returns all parts, laid end to end along the dimension named above; an argument that names none is the same for every part. Nothing has to cross between parts.
Inputs may be any that keep to these rules, and one draw needn't show every extreme that they name: `prefix_owner`: the first prefix_count[r] entries of row r, read with prefix_slot, name distinct cache blocks, at most 2 of them with one owner; in every draw some request has exactly 2 entries at every owner. Entries past the count are not read. `prefix_slot`: read with prefix_owner. `prefix_count`: some request has 8. `new_length`: some request has 1024. `at_q`: Real-valued entries. `kv_cache`: Real-valued entries.
All inputs are finite; a program needn't handle non-finite values.
Results may differ from the reference program's by a relative error of at most 0.0057.
Values may be sent and summed in bfloat16 or wider, within the bound.
No kernel may reach another device: no remote copies, remote signals or barrier semaphores. Data moves between devices by JAX's collectives and lax.ppermute only.
A program may use at most 128 MiB of HBM per device.

```python
import math
import jax
import jax.numpy as jnp
from jax import lax

HD = 128
HEADS = 32
CH = 4096
FILT = 128
BLOCK = 128
CAP = 2
BLOCKS_DEV = 4
NEWTOK = 1024
REQS = 4
MAXB = 8
CACHE = 16
QW = 4096


def prefix_lists(key):
    list_key = jax.random.fold_in(key, 17)
    slot_scores = jax.random.randint(jax.random.fold_in(list_key, 1), (REQS, REQS, BLOCKS_DEV), 0, 1048576)
    slot_scores = slot_scores * BLOCKS_DEV + jnp.arange(BLOCKS_DEV, dtype=jnp.int32)[None, None, :]
    chosen = jnp.argsort(slot_scores, axis=2)[:, :, :CAP].astype(jnp.int32)
    owner_grid = jnp.broadcast_to(jnp.arange(REQS, dtype=jnp.int32)[None, :, None], (REQS, REQS, CAP))
    order_scores = jax.random.randint(jax.random.fold_in(list_key, 2), (REQS, MAXB), 0, 1048576)
    order_scores = order_scores * MAXB + jnp.arange(MAXB, dtype=jnp.int32)[None, :]
    entry_order = jnp.argsort(order_scores, axis=1).astype(jnp.int32)
    owner_ids = jnp.take_along_axis(owner_grid.reshape(REQS, MAXB), entry_order, axis=1)
    slot_ids = jnp.take_along_axis(chosen.reshape(REQS, MAXB), entry_order, axis=1)
    return (owner_ids.astype(jnp.int32), slot_ids.astype(jnp.int32))


def draw_prefix_owner(key, part):
    return prefix_lists(key)[0]


def draw_prefix_slot(key, part):
    return prefix_lists(key)[1]


def draw_prefix_count(key, part):
    counts = jax.random.randint(jax.random.fold_in(key, 31), (REQS,), 1, MAXB + 1)
    fullest = jax.random.randint(jax.random.fold_in(key, 32), (), 0, REQS)
    return jnp.where(jnp.arange(REQS, dtype=jnp.int32) == fullest, MAXB, counts).astype(jnp.int32)


def draw_new_length(key, part):
    counts = jax.random.randint(jax.random.fold_in(key, 35), (REQS,), 1, NEWTOK + 1)
    fullest = jax.random.randint(jax.random.fold_in(key, 36), (), 0, REQS)
    return jnp.where(jnp.arange(REQS, dtype=jnp.int32) == fullest, NEWTOK, counts).astype(jnp.int32)


def draw_at_q(key, part):
    shape_all = (REQS, NEWTOK, HEADS * HD)
    drawn = jnp.clip(2.5 * jax.random.normal(jax.random.fold_in(key, 43), shape_all, jnp.float32), -12.0, 12.0)
    return drawn.astype(jnp.bfloat16)


def draw_kv_cache(key, part):
    shape_all = (CACHE, 2, BLOCK, HEADS * HD)
    drawn = jnp.clip(jax.random.normal(jax.random.fold_in(key, 47), shape_all, jnp.float32), -6.0, 6.0)
    return drawn.astype(jnp.bfloat16)


def levels(rng, extent, cuts, smallest, largest):
    factor_of, own = 1.0, jax.random.fold_in(rng, 6)
    for dim, parts in cuts:
        heights = jnp.exp(jax.random.uniform(jax.random.fold_in(own, dim), (parts,), jnp.float32, smallest / len(cuts), largest / len(cuts)))
        factor_of = factor_of * jnp.repeat(heights, extent[dim] // parts).reshape([-1 if axis == dim else 1 for axis in range(len(extent))])
    return factor_of


def normal_values(own_key, dims, width, most, cuts=(), kind=jnp.bfloat16):
    values = width * jax.random.normal(own_key, dims, jnp.float32)
    if cuts:
        values = values * levels(own_key, dims, cuts, -0.22, 0.18)
    return jnp.clip(values, -most, most).astype(kind)


def setup_inputs(seed: int = 0, part: int = 0) -> dict:
    arg_keys = jax.random.split(jax.random.key(seed), 15)
    part_splits = jax.random.split(jax.random.fold_in(arg_keys[14], part), 15)
    return {
        "hy_q": normal_values(part_splits[0], (REQS, NEWTOK, CH), 1.0, 6.0, ((0, 4), (2, 4))),
        "hy_k": normal_values(part_splits[1], (REQS, NEWTOK, CH), 1.0, 6.0, ((0, 4), (2, 4))),
        "hy_v": normal_values(part_splits[2], (REQS, NEWTOK, CH), 1.0, 6.0, ((0, 4), (2, 4))),
        "filter_taps": normal_values(arg_keys[3], (CH, FILT), 0.15, 0.8984375, ((0, 4), (1, 4))),
        "filter_decay": jnp.clip(jnp.exp(math.log(0.08) - 3.2834143 * jax.random.uniform(arg_keys[4], (CH,), jnp.float32) ** levels(arg_keys[4], (CH,), ((0, 4),), -0.2, 0.2)), 0.003, 0.08),
        "hy_cache": normal_values(part_splits[5], (CACHE, BLOCK, CH), 1.0, 6.0, ((0, 4), (2, 4))),
        "at_q": draw_at_q(jax.random.fold_in(jax.random.fold_in(arg_keys[14], part), 71), part),
        "at_k": normal_values(part_splits[7], (REQS, NEWTOK, QW), 1.0, 6.0, ((0, 4), (2, 4))),
        "at_v": normal_values(part_splits[8], (REQS, NEWTOK, QW), 1.0, 6.0, ((0, 4), (2, 4))),
        "kv_cache": draw_kv_cache(jax.random.fold_in(jax.random.fold_in(arg_keys[14], part), 71), part),
        "prefix_owner": draw_prefix_owner(jax.random.fold_in(jax.random.fold_in(arg_keys[14], part), 71), part),
        "prefix_slot": draw_prefix_slot(jax.random.fold_in(jax.random.fold_in(arg_keys[14], part), 71), part),
        "prefix_count": draw_prefix_count(jax.random.fold_in(jax.random.fold_in(arg_keys[14], part), 71), part),
        "new_length": draw_new_length(jax.random.fold_in(jax.random.fold_in(arg_keys[14], part), 71), part),
    }


def causal_filter(extended, kernel):
    kernel_wide = kernel.astype(jnp.float32)
    extended_wide = extended.astype(jnp.float32)
    total = jnp.zeros((extended.shape[0], NEWTOK, extended.shape[2]), jnp.float32)

    def add_tap(lag, acc):
        lag_index = jnp.asarray(lag).astype(jnp.int32)
        window = lax.dynamic_slice_in_dim(extended_wide, (BLOCK - lag_index).astype(jnp.int32), NEWTOK, 1)
        column = lax.dynamic_slice_in_dim(kernel_wide, lag_index, 1, 1)[:, 0]
        return acc + window * column[None, None, :]
    return lax.fori_loop(0, FILT, add_tap, total)

def reference(hy_q, hy_k, hy_v, filter_taps, filter_decay, hy_cache, at_q, at_k, at_v, kv_cache, prefix_owner, prefix_slot, prefix_count, new_length):
    positions = jnp.arange(NEWTOK, dtype=jnp.int32)
    row_live = positions[None, :] < new_length[:, None]
    last_entry = (prefix_count - 1)[:, None]
    last_block = (jnp.take_along_axis(prefix_owner, last_entry, axis=1) * BLOCKS_DEV + jnp.take_along_axis(prefix_slot, last_entry, axis=1))[:, 0]
    prior_state = hy_cache[last_block]
    gated = (hy_k.astype(jnp.float32) * hy_v.astype(jnp.float32)).astype(jnp.bfloat16)
    lag_steps = jnp.arange(FILT, dtype=jnp.float32)
    kernel = (filter_taps.astype(jnp.float32) * jnp.exp(-filter_decay[:, None] * lag_steps[None, :])).astype(jnp.bfloat16)
    extended = jnp.concatenate([prior_state, gated], axis=1)
    mixed_sum = causal_filter(extended, kernel)
    hy_out = jnp.where(row_live[:, :, None], hy_q.astype(jnp.float32) * mixed_sum, 0.0).astype(jnp.bfloat16)
    score_scale = 1.0 / math.sqrt(HD)
    prefix_rows = MAXB * BLOCK
    fresh_visible = positions[None, :] <= positions[:, None]

    def attend_request(operands):
        queries, fresh_keys, fresh_values, owners_row, slots_row, count, length = operands
        block_ids = owners_row * BLOCKS_DEV + slots_row
        listed = kv_cache[block_ids]
        entry_live = jnp.arange(MAXB, dtype=jnp.int32) < count
        key_rows = jnp.concatenate([listed[:, 0].reshape(prefix_rows, QW), fresh_keys], axis=0)
        value_rows = jnp.concatenate([listed[:, 1].reshape(prefix_rows, QW), fresh_values], axis=0)
        prefix_visible = jnp.broadcast_to(jnp.repeat(entry_live, BLOCK)[None, :], (NEWTOK, prefix_rows))
        visible = jnp.concatenate([prefix_visible, fresh_visible], axis=1)

        def attend_head(head):
            q_head = lax.dynamic_slice_in_dim(queries, head * HD, HD, 1)
            k_head = lax.dynamic_slice_in_dim(key_rows, head * HD, HD, 1)
            v_head = lax.dynamic_slice_in_dim(value_rows, head * HD, HD, 1)
            scores = jnp.dot(q_head, k_head.T, preferred_element_type=jnp.float32) * score_scale
            scores = jnp.where(visible, scores, -jnp.inf)
            top = lax.optimization_barrier(jnp.max(scores, axis=1))
            expo = jnp.exp(scores - top[:, None])
            weights = expo.astype(jnp.bfloat16)
            numer = jnp.dot(weights, v_head, preferred_element_type=jnp.float32)
            return numer / lax.optimization_barrier(jnp.sum(expo, axis=1))[:, None]
        per_head = lax.map(attend_head, jnp.arange(HEADS, dtype=jnp.int32))
        joined = jnp.transpose(per_head, (1, 0, 2)).reshape(NEWTOK, QW)
        return jnp.where((positions < length)[:, None], joined, 0.0).astype(jnp.bfloat16)
    at_out = lax.map(attend_request, (at_q, at_k, at_v, prefix_owner, prefix_slot, prefix_count, new_length))
    return (hy_out, at_out)
```

```python
import functools
import math

import jax
import jax.numpy as jnp
import numpy as np
from jax import lax
from jax.experimental import pallas as pl
from jax.experimental.pallas import tpu as pltpu
from jax.sharding import PartitionSpec as P

HD = 128
CAP = 2
LOG2E = 1.4426950408889634
NEG = -1e30


def dft_matrices(size):
    window = 2 * size
    freq = np.arange(size)[:, None] + 0.5
    time = np.arange(window)[None, :]
    angle = 2.0 * np.pi * freq * time / window
    forward = np.concatenate([np.cos(angle), -np.sin(angle)], axis=0)
    inverse = forward[:, size:].T / size

    def split(matrix):
        high = matrix.astype(jnp.bfloat16)
        low = (matrix - high.astype(np.float64)).astype(jnp.bfloat16)
        return np.stack([high, low])

    return split(forward), split(inverse)


def hyena_kernel(s_ref, q_ref, k_ref, v_ref, *rest):
    *prior_refs, taps_ref, decay_ref, fwd_ref, inv_ref, o_ref = rest
    sources = len(prior_refs)
    new_length = s_ref[0]
    source = s_ref[1]
    size = inv_ref.shape[1]
    width = q_ref.shape[2]
    f32 = jnp.float32
    dot = functools.partial(jnp.dot, preferred_element_type=f32)
    pieces = taps_ref.shape[0]
    order = 2 + sources
    taps = jnp.concatenate([taps_ref[s_ref[order + j]] for j in range(pieces)], axis=0)
    lag = lax.broadcasted_iota(jnp.int32, (size, width), 0)
    kern = (taps.astype(f32) * jnp.exp(-decay_ref[...] * lag.astype(f32))).astype(jnp.bfloat16)
    spectrum = dot(fwd_ref[0, :, :size], kern) + dot(fwd_ref[1, :, :size], kern)
    kr, ki = spectrum[:size], spectrum[size:]
    prev = prior_refs[0][0]
    for i in range(1, sources):
        prev = jnp.where(source == i, prior_refs[i][0], prev)
    for b in range(q_ref.shape[1] // size):
        rows = pl.ds(b * size, size)
        cur = (k_ref[0, rows, :].astype(f32) * v_ref[0, rows, :].astype(f32)).astype(jnp.bfloat16)
        live = b * size < new_length

        @pl.when(live)
        def _(prev=prev, cur=cur, rows=rows, b=b):
            window = jnp.concatenate([prev, cur], axis=0)
            x = dot(fwd_ref[0], window) + dot(fwd_ref[1], window)
            xr, xi = x[:size], x[size:]
            y = jnp.concatenate([xr * kr - xi * ki, xr * ki + xi * kr], axis=0)
            y_high = y.astype(jnp.bfloat16)
            y_low = (y - y_high.astype(f32)).astype(jnp.bfloat16)
            mixed = dot(inv_ref[0], y_high) + dot(inv_ref[0], y_low) + dot(inv_ref[1], y_high)
            out = q_ref[0, rows, :].astype(f32) * mixed
            o_ref[0, rows, :] = jnp.where(lag + b * size < new_length, out, 0.0).astype(o_ref.dtype)

        @pl.when(jnp.logical_not(live))
        def _(rows=rows):
            o_ref[0, rows, :] = jnp.zeros((size, width), o_ref.dtype)

        prev = cur


def hyena(scalars, hy_q, hy_k, hy_v, priors, taps, decay):
    rows, channels = hy_q.shape[1:]
    size = priors[0].shape[1]
    tile = math.gcd(channels, 256)
    forward, inverse = dft_matrices(size)
    row_spec = pl.BlockSpec((1, rows, tile), lambda c, s: (0, 0, c))

    def prior_spec(i):
        return pl.BlockSpec((1, size, tile), lambda c, s: (s[2 + i], 0, c))

    blocks = rows // size
    return pl.pallas_call(
        hyena_kernel,
        name="hyena",
        grid_spec=pltpu.PrefetchScalarGridSpec(
            num_scalar_prefetch=1,
            grid=(channels // tile,),
            in_specs=[row_spec] * 3
            + [prior_spec(i) for i in range(len(priors))]
            + [
                pl.BlockSpec((*taps.shape[:2], tile), lambda c, s: (0, 0, c)),
                pl.BlockSpec((1, tile), lambda c, s: (0, c)),
                pl.BlockSpec(forward.shape, lambda c, s: (0, 0, 0)),
                pl.BlockSpec(inverse.shape, lambda c, s: (0, 0, 0)),
            ],
            out_specs=row_spec,
        ),
        out_shape=jax.ShapeDtypeStruct(hy_q.shape, hy_q.dtype),
        compiler_params=pltpu.CompilerParams(vmem_limit_bytes=24 << 20),
        cost_estimate=pl.CostEstimate(
            flops=blocks * channels * size * size * 30, bytes_accessed=8 * rows * channels, transcendentals=size * channels
        ),
    )(scalars, hy_q, hy_k, hy_v, *priors, taps, decay[None, :], jnp.asarray(forward), jnp.asarray(inverse))


def attend_kernel(fresh, pairs, carried, final, s_ref, *refs):
    refs = list(refs)
    q_ref = refs.pop(0)
    fk_ref, fv_ref = (refs.pop(0), refs.pop(0)) if fresh else (None, None)
    blocks = [refs.pop(0) for _ in range(2 * pairs)]
    o_in, lse_in = (refs.pop(0), refs.pop(0)) if carried else (None, None)
    o_ref = refs.pop(0)
    lse_ref = None if final else refs.pop(0)
    m_ref, l_ref, acc_ref = refs
    rows = q_ref.shape[1]
    tile = math.gcd(rows, 256)
    new_length = s_ref[0]
    scale = LOG2E / math.sqrt(HD)
    f32 = jnp.float32

    def fold(queries, keys, values, visible, first):
        scores = lax.dot_general(queries, keys, (((1,), (1,)), ((), ())), preferred_element_type=f32) * scale
        if visible is not None:
            scores = jnp.where(visible, scores, NEG)
        top = jnp.max(scores, axis=1, keepdims=True)
        if not first:
            top = jnp.maximum(top, m_ref[...])
        expo = jnp.exp2(scores - top)
        total = jnp.sum(expo, axis=1, keepdims=True)
        numer = jnp.dot(expo.astype(jnp.bfloat16), values, preferred_element_type=f32)
        if not first:
            shrink = jnp.exp2(m_ref[...] - top)
            total = total + l_ref[...] * shrink
            numer = numer + acc_ref[...] * shrink
        m_ref[...] = top
        l_ref[...] = total
        acc_ref[...] = numer

    for i in range(rows // tile):
        span = pl.ds(i * tile, tile)

        @pl.when(i * tile < new_length)
        def _(i=i, span=span):
            queries = q_ref[0, span, :]
            if carried:
                m_ref[...] = lse_in[0, span, :1]
                l_ref[...] = jnp.ones_like(l_ref)
                acc_ref[...] = o_in[0, span, :]
            if fresh:
                row = lax.broadcasted_iota(jnp.int32, (tile, tile), 0)
                col = lax.broadcasted_iota(jnp.int32, (tile, tile), 1)
                fold(queries, fk_ref[0, span, :], fv_ref[0, span, :], col <= row, not carried)
                if i:
                    ahead = pl.ds(0, i * tile)
                    fold(queries, fk_ref[0, ahead, :], fv_ref[0, ahead, :], None, False)
            for j in range(pairs):
                live_a, live_b = s_ref[1 + 2 * pairs + 2 * j], s_ref[2 + 2 * pairs + 2 * j]

                @pl.when(live_a + live_b > 0)
                def _(j=j, live_a=live_a, live_b=live_b):
                    a, b = blocks[2 * j], blocks[2 * j + 1]
                    keys = jnp.concatenate([a[0, 0], b[0, 0]], axis=0)
                    values = jnp.concatenate([a[0, 1], b[0, 1]], axis=0)
                    col = lax.broadcasted_iota(jnp.int32, (1, keys.shape[0]), 1)
                    visible = jnp.where(col < a.shape[2], live_a, live_b) > 0
                    fold(queries, keys, values, visible, False)

            result = acc_ref[...] / l_ref[...]
            if final:
                row = lax.broadcasted_iota(jnp.int32, (tile, HD), 0) + i * tile
                o_ref[0, span, :] = jnp.where(row < new_length, result, 0.0).astype(o_ref.dtype)
            else:
                o_ref[0, span, :] = result
                lse_ref[0, span, :] = jnp.broadcast_to(m_ref[...] + jnp.log2(l_ref[...]), (tile, HD))

        if final:

            @pl.when(i * tile >= new_length)
            def _(span=span):
                o_ref[0, span, :] = jnp.zeros((tile, HD), o_ref.dtype)


def attend(new_length, queries, fresh, blocks, carry, final):
    rows, width = queries.shape[1:]
    heads = width // HD
    pairs = len(blocks) // 2
    tile = math.gcd(rows, 256)
    scalars = jnp.stack(
        [new_length] + [index for _, index, _ in blocks] + [live.astype(jnp.int32) for _, _, live in blocks]
    ).astype(jnp.int32)
    row_spec = pl.BlockSpec((1, rows, HD), lambda h, s: (0, 0, h))

    def block_spec(i, array):
        return pl.BlockSpec((1, 2, array.shape[2], HD), lambda h, s: (s[1 + i], 0, 0, h))

    operands = [queries]
    in_specs = [row_spec]
    if fresh is not None:
        operands += fresh
        in_specs += [row_spec] * 2
    for i, (array, _, _) in enumerate(blocks):
        operands.append(array)
        in_specs.append(block_spec(i, array))
    if carry is not None:
        operands += carry
        in_specs += [row_spec] * 2
    keys = sum(array.shape[2] for array, _, _ in blocks) + (rows // 2 if fresh is not None else 0)
    if final:
        out_shape = jax.ShapeDtypeStruct(queries.shape, queries.dtype)
        out_specs = row_spec
    else:
        out_shape = [jax.ShapeDtypeStruct(queries.shape, jnp.float32)] * 2
        out_specs = [row_spec] * 2
    return pl.pallas_call(
        functools.partial(attend_kernel, fresh is not None, pairs, carry is not None, final),
        name="attend",
        grid_spec=pltpu.PrefetchScalarGridSpec(
            num_scalar_prefetch=1,
            grid=(heads,),
            in_specs=in_specs,
            out_specs=out_specs,
            scratch_shapes=[
                pltpu.VMEM((tile, 1), jnp.float32),
                pltpu.VMEM((tile, 1), jnp.float32),
                pltpu.VMEM((tile, HD), jnp.float32),
            ],
        ),
        out_shape=out_shape,
        compiler_params=pltpu.CompilerParams(vmem_limit_bytes=24 << 20),
        cost_estimate=pl.CostEstimate(
            flops=16 * rows * keys * width, bytes_accessed=8 * rows * width, transcendentals=rows * keys * heads
        ),
    )(scalars, *operands)


def per_device(
    hy_q, hy_k, hy_v, filter_taps, filter_decay, hy_cache, at_q, at_k, at_v, kv_cache,
    prefix_owner, prefix_slot, prefix_count, new_length,
):
    me = lax.axis_index("req")
    requests, entries = prefix_owner.shape
    length = new_length[0]

    entry = jnp.arange(entries, dtype=jnp.int32)
    live = entry[None, :] < prefix_count[:, None]
    same = jnp.logical_and(live[:, None, :], prefix_owner[:, :, None] == prefix_owner[:, None, :])
    rank = jnp.sum(jnp.where(entry[None, None, :] < entry[None, :, None], same, False).astype(jnp.int32), axis=2)
    owners = jnp.arange(requests, dtype=jnp.int32)
    owned = jnp.logical_and(live[:, None, :], prefix_owner[:, None, :] == owners[None, :, None])
    places = jnp.arange(CAP, dtype=jnp.int32)
    choose = jnp.logical_and(owned[:, :, None, :], rank[:, None, None, :] == places[None, None, :, None])
    slots = jnp.sum(jnp.where(choose, prefix_slot[:, None, None, :], 0), axis=3)
    counts = jnp.sum(owned.astype(jnp.int32), axis=2)
    at_last = entry[None, :] == prefix_count[:, None] - 1
    last_owner = jnp.sum(jnp.where(at_last, prefix_owner, 0), axis=1)
    last_slot = jnp.sum(jnp.where(at_last, prefix_slot, 0), axis=1)

    def pick(array, index):
        return lax.dynamic_index_in_dim(array, index, 0, keepdims=False)

    my_counts = pick(counts, me)
    my_slots = pick(slots, me)
    my_last_owner = pick(last_owner, me)
    my_last_slot = pick(last_slot, me)
    my_taps = filter_taps.T

    def permute(array, flip):
        return lax.ppermute(array, "req", [(r, r ^ flip) for r in range(requests)])

    def send(flip):
        return permute(kv_cache[pick(pick(slots, me ^ flip), me)], flip)

    zero = jnp.int32(0)
    mate_hy = permute(hy_cache, 1)
    dst_owner, dst_slot = pick(last_owner, me ^ 2), pick(last_slot, me ^ 2)
    crossing = jnp.where(dst_owner == me, pick(hy_cache, dst_slot), pick(mate_hy, dst_slot))
    from_cross = permute(crossing[None], 2)
    mate = send(1)
    cross = send(2)
    diagonal = send(3)
    taps = lax.all_gather(my_taps, "req", axis=0)

    def pair(array, owner, indices):
        return [(array, indices[i], i < pick(my_counts, owner)) for i in range(CAP)]

    local = (zero, zero + 1)
    carry = attend(length, at_q, (at_k, at_v), pair(kv_cache, me, pick(my_slots, me)), None, False)
    source = jnp.where(my_last_owner == me, 0, jnp.where(my_last_owner == (me ^ 1), 1, 2))
    hy_scalars = jnp.concatenate(
        [jnp.stack([length, source, my_last_slot, my_last_slot, zero]), jnp.arange(requests, dtype=jnp.int32)]
    )
    hy_out = hyena(hy_scalars, hy_q, hy_k, hy_v, (hy_cache, mate_hy, from_cross), taps, filter_decay)
    carry = attend(length, at_q, None, pair(mate, me ^ 1, local) + pair(cross, me ^ 2, local), carry, False)
    at_out = attend(length, at_q, None, pair(diagonal, me ^ 3, local), carry, True)
    return hy_out, at_out


def per_device_general(
    hy_q, hy_k, hy_v, filter_taps, filter_decay, hy_cache, at_q, at_k, at_v, kv_cache,
    prefix_owner, prefix_slot, prefix_count, new_length,
):
    me = lax.axis_index("req")
    requests, entries = prefix_owner.shape
    length = new_length[0]
    entry = jnp.arange(entries, dtype=jnp.int32)
    live = entry[None, :] < prefix_count[:, None]
    mine = jnp.logical_and(live, prefix_owner == me)
    rank = jnp.cumsum(mine.astype(jnp.int32), axis=1) - mine.astype(jnp.int32)
    places = jnp.arange(CAP, dtype=jnp.int32)
    choose = jnp.logical_and(mine[:, None, :], rank[:, None, :] == places[None, :, None])
    send_slots = jnp.sum(jnp.where(choose, prefix_slot[:, None, :], 0), axis=2)
    at_last = entry[None, :] == prefix_count[:, None] - 1
    last_slot = jnp.sum(jnp.where(at_last, prefix_slot, 0), axis=1)
    last_owner = jnp.sum(jnp.where(at_last, prefix_owner, 0), axis=1)[me]
    my_owners = jnp.where(live[me], prefix_owner[me], -1)
    owners = jnp.arange(requests, dtype=jnp.int32)
    my_counts = jnp.sum((my_owners[None, :] == owners[:, None]).astype(jnp.int32), axis=1)
    incoming_hy = lax.all_to_all(hy_cache[last_slot], "req", 0, 0, tiled=True)
    incoming = lax.all_to_all(kv_cache[send_slots], "req", 0, 0, tiled=True)
    incoming = incoming.reshape(requests * CAP, *kv_cache.shape[1:])
    taps = lax.all_gather(filter_taps.T, "req", axis=0)
    carry = attend(length, at_q, (at_k, at_v), [], None, False)
    zero = jnp.int32(0)
    hy_scalars = jnp.concatenate([jnp.stack([length, zero, last_owner]), owners])
    hy_out = hyena(hy_scalars, hy_q, hy_k, hy_v, (incoming_hy,), taps, filter_decay)
    blocks = [
        (incoming, jnp.int32(owner * CAP + i), i < my_counts[owner]) for owner in range(requests) for i in range(CAP)
    ]
    return hy_out, attend(length, at_q, None, blocks, carry, True)


def solution(mesh):
    rows = P(("grp", "req"), None, "fsdp")
    placed = (
        rows, rows, rows, P("fsdp", "req"), P("fsdp"), rows, rows, rows, rows,
        P(("grp", "req"), None, None, "fsdp"), P("grp", None), P("grp", None), P("grp"), P(("grp", "req")),
    )
    body = per_device if mesh.shape["req"] == 4 else per_device_general
    return jax.shard_map(body, mesh=mesh, in_specs=placed, out_specs=(rows, rows), check_vma=False)
```

```python
import functools
import math

import jax
import jax.numpy as jnp
import numpy as np
from jax import lax
from jax.experimental import pallas as pl
from jax.experimental.pallas import tpu as pltpu
from jax.sharding import PartitionSpec as P

HD = 128
CAP = 2
LOG2E = 1.4426950408889634
NEG = -1e30
VMEM_LIMIT = 58 << 20


def dft_matrices(size):
    window = 2 * size
    freq = np.arange(size)[:, None] + 0.5
    time = np.arange(window)[None, :]
    angle = 2.0 * np.pi * freq * time / window
    forward = np.concatenate([np.cos(angle), -np.sin(angle)], axis=0)
    inverse = forward[:, size:].T / size

    def split(matrix):
        high = matrix.astype(jnp.bfloat16)
        low = (matrix - high.astype(np.float64)).astype(jnp.bfloat16)
        return np.stack([high, low])

    return split(forward), split(inverse)


def hyena_kernel(s_ref, q_ref, k_ref, v_ref, *rest):
    *prior_refs, taps_ref, decay_ref, fwd_ref, inv_ref, o_ref = rest
    sources = len(prior_refs)
    new_length = s_ref[0]
    source = s_ref[1]
    size = inv_ref.shape[1]
    width = q_ref.shape[2]
    f32 = jnp.float32
    dot = functools.partial(jnp.dot, preferred_element_type=f32)
    pieces = taps_ref.shape[0]
    order = 2 + sources
    taps = jnp.concatenate([taps_ref[s_ref[order + j]] for j in range(pieces)], axis=0)
    lag = lax.broadcasted_iota(jnp.int32, (size, width), 0)
    kern = (taps.astype(f32) * jnp.exp(-decay_ref[...] * lag.astype(f32))).astype(jnp.bfloat16)
    spectrum = dot(fwd_ref[0, :, :size], kern) + dot(fwd_ref[1, :, :size], kern)
    kr, ki = spectrum[:size], spectrum[size:]
    prev = prior_refs[0][0]
    for i in range(1, sources):
        prev = jnp.where(source == i, prior_refs[i][0], prev)
    for b in range(q_ref.shape[1] // size):
        rows = pl.ds(b * size, size)
        cur = (k_ref[0, rows, :].astype(f32) * v_ref[0, rows, :].astype(f32)).astype(jnp.bfloat16)
        live = b * size < new_length

        @pl.when(live)
        def _(prev=prev, cur=cur, rows=rows, b=b):
            window = jnp.concatenate([prev, cur], axis=0)
            x = dot(fwd_ref[0], window) + dot(fwd_ref[1], window)
            xr, xi = x[:size], x[size:]
            y = jnp.concatenate([xr * kr - xi * ki, xr * ki + xi * kr], axis=0)
            y_high = y.astype(jnp.bfloat16)
            y_low = (y - y_high.astype(f32)).astype(jnp.bfloat16)
            mixed = dot(inv_ref[0], y_high) + dot(inv_ref[0], y_low) + dot(inv_ref[1], y_high)
            out = q_ref[0, rows, :].astype(f32) * mixed
            o_ref[0, rows, :] = jnp.where(lag + b * size < new_length, out, 0.0).astype(o_ref.dtype)

        @pl.when(jnp.logical_not(live))
        def _(rows=rows):
            o_ref[0, rows, :] = jnp.zeros((size, width), o_ref.dtype)

        prev = cur


def hyena(scalars, hy_q, hy_k, hy_v, priors, taps, decay):
    rows, channels = hy_q.shape[1:]
    size = priors[0].shape[1]
    tile = math.gcd(channels, 256)
    forward, inverse = dft_matrices(size)
    row_spec = pl.BlockSpec((1, rows, tile), lambda c, s: (0, 0, c))

    def prior_spec(i):
        return pl.BlockSpec((1, size, tile), lambda c, s: (s[2 + i], 0, c))

    blocks = rows // size
    return pl.pallas_call(
        hyena_kernel,
        name="hyena",
        grid_spec=pltpu.PrefetchScalarGridSpec(
            num_scalar_prefetch=1,
            grid=(channels // tile,),
            in_specs=[row_spec] * 3
            + [prior_spec(i) for i in range(len(priors))]
            + [
                pl.BlockSpec((*taps.shape[:2], tile), lambda c, s: (0, 0, c)),
                pl.BlockSpec((1, tile), lambda c, s: (0, c)),
                pl.BlockSpec(forward.shape, lambda c, s: (0, 0, 0)),
                pl.BlockSpec(inverse.shape, lambda c, s: (0, 0, 0)),
            ],
            out_specs=row_spec,
        ),
        out_shape=jax.ShapeDtypeStruct(hy_q.shape, hy_q.dtype),
        compiler_params=pltpu.CompilerParams(vmem_limit_bytes=VMEM_LIMIT),
        cost_estimate=pl.CostEstimate(
            flops=blocks * channels * size * size * 30, bytes_accessed=8 * rows * channels, transcendentals=size * channels
        ),
    )(scalars, hy_q, hy_k, hy_v, *priors, taps, decay[None, :], jnp.asarray(forward), jnp.asarray(inverse))


def attend_kernel(query_tile, fresh, count, carried, final, s_ref, *refs):
    refs = list(refs)
    q_ref = refs.pop(0)
    fk_ref, fv_ref = (refs.pop(0), refs.pop(0)) if fresh else (None, None)
    blocks = [refs.pop(0) for _ in range(count)]
    acc_in, stat_in = (refs.pop(0), refs.pop(0)) if carried else (None, None)
    o_ref = refs.pop(0)
    stat_ref = None if final else refs.pop(0)
    rows, width = q_ref.shape[1:]
    tile = math.gcd(rows, query_tile)
    new_length = s_ref[0]
    scale = LOG2E / math.sqrt(HD)
    f32 = jnp.float32
    lives = [s_ref[1 + count + j] for j in range(count)]

    def score(keys, queries):
        return lax.dot_general(keys, queries, (((1,), (1,)), ((), ())), preferred_element_type=f32)

    for h in range(width // HD):
        cols = slice(h * HD, (h + 1) * HD)
        if fresh:
            fresh_values = fv_ref[0, :, cols].T
        if count:
            size = blocks[0].shape[2]
            cached_keys = jnp.concatenate([b[0, 0, :, cols] for b in blocks], axis=0)
            cached_values = jnp.concatenate([b[0, 1, :, cols].T for b in blocks], axis=1)
        for i in range(rows // tile):
            span = slice(i * tile, (i + 1) * tile)
            queries = q_ref[0, span, cols]
            parts = []
            if fresh:
                if i:
                    parts.append((score(fk_ref[0, : i * tile, cols], queries), fresh_values[:, : i * tile]))
                key = lax.broadcasted_iota(jnp.int32, (tile, tile), 0)
                col = lax.broadcasted_iota(jnp.int32, (tile, tile), 1)
                diagonal = jnp.where(key <= col, score(fk_ref[0, span, cols], queries), NEG)
                parts.append((diagonal, fresh_values[:, span]))
            if count:
                scores = score(cached_keys, queries)
                scores = jnp.concatenate(
                    [jnp.where(lives[j] > 0, scores[j * size : (j + 1) * size], NEG) for j in range(count)], axis=0
                )
                parts.append((scores, cached_values))
            tops = [jnp.max(scores, axis=0, keepdims=True) for scores, _ in parts]
            if carried:
                tops.append(stat_in[h, :1, span])
            top = functools.reduce(jnp.maximum, tops)
            top_scaled = top * scale
            if carried:
                shrink = jnp.exp2(stat_in[h, :1, span] * scale - top_scaled)
                total = stat_in[h, 1:, span] * shrink
                acc = acc_in[cols, span] * shrink
            else:
                total, acc = 0.0, 0.0
            for scores, values in parts:
                expo = jnp.exp2(scores * scale - top_scaled)
                total = total + jnp.sum(expo, axis=0, keepdims=True)
                acc = acc + jnp.dot(values, expo.astype(jnp.bfloat16), preferred_element_type=f32)
            if final:
                result = acc * (1.0 / total)
                lane = lax.broadcasted_iota(jnp.int32, (HD, tile), 1) + i * tile
                o_ref[0, span, cols] = jnp.where(lane < new_length, result, 0.0).T.astype(o_ref.dtype)
            else:
                o_ref[cols, span] = acc
                stat_ref[h, :1, span] = top
                stat_ref[h, 1:, span] = total


def attend(new_length, queries, fresh, blocks, carry, final):
    scalars = jnp.stack(
        [new_length] + [index for _, index, _ in blocks] + [live.astype(jnp.int32) for _, _, live in blocks]
    ).astype(jnp.int32)
    blocks = [array for array, _, _ in blocks]
    rows, width = queries.shape[1:]
    heads = width // HD
    group = math.gcd(heads, 2)
    count = len(blocks)
    row_spec = pl.BlockSpec((1, rows, group * HD), lambda h, s: (0, 0, h))
    carry_specs = [
        pl.BlockSpec((group * HD, rows), lambda h, s: (h, 0)),
        pl.BlockSpec((group, 2, rows), lambda h, s: (h, 0, 0)),
    ]

    def block_spec(i, array):
        return pl.BlockSpec((1, 2, array.shape[2], group * HD), lambda h, s: (s[1 + i], 0, 0, h))

    operands = [queries]
    in_specs = [row_spec]
    if fresh is not None:
        operands += fresh
        in_specs += [row_spec] * 2
    for i, array in enumerate(blocks):
        operands.append(array)
        in_specs.append(block_spec(i, array))
    if carry is not None:
        operands += carry
        in_specs += carry_specs
    cached = sum(array.shape[2] for array in blocks)
    keys = cached + (rows // 2 if fresh is not None else 0)
    if final:
        out_shape = jax.ShapeDtypeStruct(queries.shape, queries.dtype)
        out_specs = row_spec
    else:
        out_shape = [
            jax.ShapeDtypeStruct((width, rows), jnp.float32),
            jax.ShapeDtypeStruct((heads, 2, rows), jnp.float32),
        ]
        out_specs = carry_specs
    return pl.pallas_call(
        functools.partial(attend_kernel, 1024 if fresh is None else 512, fresh is not None, count, carry is not None, final),
        name="attend",
        grid_spec=pltpu.PrefetchScalarGridSpec(
            num_scalar_prefetch=1, grid=(heads // group,), in_specs=in_specs, out_specs=out_specs
        ),
        out_shape=out_shape,
        compiler_params=pltpu.CompilerParams(vmem_limit_bytes=VMEM_LIMIT),
        cost_estimate=pl.CostEstimate(
            flops=4 * rows * keys * width, bytes_accessed=8 * rows * width, transcendentals=rows * keys * heads
        ),
    )(scalars, *operands)


def per_device(
    hy_q, hy_k, hy_v, filter_taps, filter_decay, hy_cache, at_q, at_k, at_v, kv_cache,
    prefix_owner, prefix_slot, prefix_count, new_length,
):
    me = lax.axis_index("req")
    requests, entries = prefix_owner.shape
    length = new_length[0]

    entry = jnp.arange(entries, dtype=jnp.int32)
    live = entry[None, :] < prefix_count[:, None]
    same = jnp.logical_and(live[:, None, :], prefix_owner[:, :, None] == prefix_owner[:, None, :])
    rank = jnp.sum(jnp.where(entry[None, None, :] < entry[None, :, None], same, False).astype(jnp.int32), axis=2)
    owners = jnp.arange(requests, dtype=jnp.int32)
    owned = jnp.logical_and(live[:, None, :], prefix_owner[:, None, :] == owners[None, :, None])
    places = jnp.arange(CAP, dtype=jnp.int32)
    choose = jnp.logical_and(owned[:, :, None, :], rank[:, None, None, :] == places[None, None, :, None])
    slots = jnp.sum(jnp.where(choose, prefix_slot[:, None, None, :], 0), axis=3)
    counts = jnp.sum(owned.astype(jnp.int32), axis=2)
    at_last = entry[None, :] == prefix_count[:, None] - 1
    last_owner = jnp.sum(jnp.where(at_last, prefix_owner, 0), axis=1)
    last_slot = jnp.sum(jnp.where(at_last, prefix_slot, 0), axis=1)

    def pick(array, index):
        return lax.dynamic_index_in_dim(array, index, 0, keepdims=False)

    my_counts = pick(counts, me)
    my_slots = pick(slots, me)
    my_last_owner = pick(last_owner, me)
    my_last_slot = pick(last_slot, me)
    my_taps = filter_taps.T

    def permute(array, flip):
        return lax.ppermute(array, "req", [(r, r ^ flip) for r in range(requests)])

    def send(flip):
        return permute(kv_cache[pick(pick(slots, me ^ flip), me)], flip)

    zero = jnp.int32(0)
    mate_hy = permute(hy_cache, 1)
    taps_pair = jnp.stack([my_taps, permute(my_taps, 2)])
    taps = jnp.concatenate([taps_pair, permute(taps_pair, 1)])
    dst_owner, dst_slot = pick(last_owner, me ^ 2), pick(last_slot, me ^ 2)
    crossing = jnp.where(dst_owner == me, pick(hy_cache, dst_slot), pick(mate_hy, dst_slot))
    from_cross = permute(crossing[None], 2)
    mate = send(1)
    cross = send(2)
    diagonal = send(3)

    def pair(array, owner, indices):
        return [(array, indices[i], i < pick(my_counts, owner)) for i in range(CAP)]

    local = (zero, zero + 1)
    carry = attend(length, at_q, (at_k, at_v), pair(kv_cache, me, pick(my_slots, me)), None, False)
    source = jnp.where(my_last_owner == me, 0, jnp.where(my_last_owner == (me ^ 1), 1, 2))
    hy_scalars = jnp.concatenate(
        [jnp.stack([length, source, my_last_slot, my_last_slot, zero]), jnp.asarray([0, 2, 1, 3])[owners ^ me]]
    )
    hy_out = hyena(hy_scalars, hy_q, hy_k, hy_v, (hy_cache, mate_hy, from_cross), taps, filter_decay)
    hy_out, carry = lax.optimization_barrier((hy_out, carry))
    carry = attend(length, at_q, None, pair(mate, me ^ 1, local) + pair(cross, me ^ 2, local), carry, False)
    at_out = attend(length, at_q, None, pair(diagonal, me ^ 3, local), carry, True)
    return hy_out, at_out


def per_device_general(
    hy_q, hy_k, hy_v, filter_taps, filter_decay, hy_cache, at_q, at_k, at_v, kv_cache,
    prefix_owner, prefix_slot, prefix_count, new_length,
):
    me = lax.axis_index("req")
    requests, entries = prefix_owner.shape
    length = new_length[0]
    entry = jnp.arange(entries, dtype=jnp.int32)
    live = entry[None, :] < prefix_count[:, None]
    mine = jnp.logical_and(live, prefix_owner == me)
    rank = jnp.cumsum(mine.astype(jnp.int32), axis=1) - mine.astype(jnp.int32)
    places = jnp.arange(CAP, dtype=jnp.int32)
    choose = jnp.logical_and(mine[:, None, :], rank[:, None, :] == places[None, :, None])
    send_slots = jnp.sum(jnp.where(choose, prefix_slot[:, None, :], 0), axis=2)
    at_last = entry[None, :] == prefix_count[:, None] - 1
    last_slot = jnp.sum(jnp.where(at_last, prefix_slot, 0), axis=1)
    last_owner = jnp.sum(jnp.where(at_last, prefix_owner, 0), axis=1)[me]
    my_owners = jnp.where(live[me], prefix_owner[me], -1)
    owners = jnp.arange(requests, dtype=jnp.int32)
    my_counts = jnp.sum((my_owners[None, :] == owners[:, None]).astype(jnp.int32), axis=1)
    incoming_hy = lax.all_to_all(hy_cache[last_slot], "req", 0, 0, tiled=True)
    incoming = lax.all_to_all(kv_cache[send_slots], "req", 0, 0, tiled=True)
    incoming = incoming.reshape(requests * CAP, *kv_cache.shape[1:])
    taps = lax.all_gather(filter_taps.T, "req", axis=0)
    carry = attend(length, at_q, (at_k, at_v), [], None, False)
    zero = jnp.int32(0)
    hy_scalars = jnp.concatenate([jnp.stack([length, zero, last_owner]), owners])
    hy_out = hyena(hy_scalars, hy_q, hy_k, hy_v, (incoming_hy,), taps, filter_decay)
    blocks = [
        (incoming, jnp.int32(owner * CAP + i), i < my_counts[owner]) for owner in range(requests) for i in range(CAP)
    ]
    return hy_out, attend(length, at_q, None, blocks, carry, True)


def solution(mesh):
    rows = P(("grp", "req"), None, "fsdp")
    placed = (
        rows, rows, rows, P("fsdp", "req"), P("fsdp"), rows, rows, rows, rows,
        P(("grp", "req"), None, None, "fsdp"), P("grp", None), P("grp", None), P("grp"), P(("grp", "req")),
    )
    body = per_device if mesh.shape["req"] == 4 else per_device_general
    return jax.shard_map(body, mesh=mesh, in_specs=placed, out_specs=(rows, rows), check_vma=False)
```

```python
import functools
import math

import jax
import jax.numpy as jnp
import numpy as np
from jax import lax
from jax.experimental import pallas as pl
from jax.experimental.pallas import tpu as pltpu
from jax.sharding import PartitionSpec as P

HD = 128
CAP = 2
LOG2E = 1.4426950408889634
NEG = -1e30
VMEM_LIMIT = 58 << 20


def dft_matrices(size):
    freq = np.arange(size)[:, None] + 0.5
    angle = np.pi * freq * np.arange(2 * size)[None, :] / size
    matrix = np.concatenate([np.cos(angle), -np.sin(angle)], axis=0)

    def split(values):
        high = values.astype(jnp.bfloat16)
        return high, (values - high.astype(np.float64)).astype(jnp.bfloat16)

    high, low = split(matrix[:, :size])
    inverse_high, inverse_low = split(matrix[:, size:].T / size)
    return np.concatenate([high, low], axis=1), np.concatenate([inverse_high, inverse_high, inverse_low], axis=1)


def hyena_kernel(prior_at, source_at, taps_at, s_ref, q_ref, k_ref, v_ref, *rest):
    *prior_refs, taps_ref, decay_ref, fwd_ref, inv_ref, o_ref = rest
    new_length = s_ref[0]
    source = s_ref[source_at]
    size = inv_ref.shape[0]
    width = q_ref.shape[2]
    f32 = jnp.float32
    taps = jnp.concatenate([taps_ref[s_ref[taps_at + j]] for j in range(taps_ref.shape[0])], axis=0)
    lag = lax.broadcasted_iota(jnp.int32, (size, width), 0)
    kern = (taps.astype(f32) * jnp.exp(-decay_ref[...] * lag.astype(f32))).astype(jnp.bfloat16)
    forward = fwd_ref[...]
    inverse = inv_ref[...]

    def transform(block):
        return jnp.dot(forward, jnp.concatenate([block, block], axis=0), preferred_element_type=f32)

    spectrum = transform(kern)
    kr, ki = spectrum[:size], spectrum[size:]
    sign = jnp.where(lag % 2 == 0, 1.0, -1.0)
    prior = prior_refs[0][0]
    for i in range(1, len(prior_refs)):
        prior = jnp.where(source == i, prior_refs[i][0], prior)
    prev = transform(prior)
    for b in range(q_ref.shape[1] // size):
        rows = slice(b * size, (b + 1) * size)
        cur = transform((k_ref[0, rows, :].astype(f32) * v_ref[0, rows, :].astype(f32)).astype(jnp.bfloat16))
        xr = prev[:size] + sign * cur[size:]
        xi = prev[size:] - sign * cur[:size]
        y = jnp.concatenate([xr * kr - xi * ki, xr * ki + xi * kr], axis=0)
        high = y.astype(jnp.bfloat16)
        low = (y - high.astype(f32)).astype(jnp.bfloat16)
        mixed = jnp.dot(inverse, jnp.concatenate([high, low, high], axis=0), preferred_element_type=f32)
        gated = q_ref[0, rows, :].astype(f32) * mixed
        o_ref[0, rows, :] = jnp.where(lag + b * size < new_length, gated, 0.0).astype(o_ref.dtype)
        prev = cur


def hyena(table, hy_q, hy_k, hy_v, priors, prior_at, source_at, taps, taps_at, decay):
    rows, channels = hy_q.shape[1:]
    size = priors[0].shape[1]
    tile = math.gcd(channels, 256)
    forward, inverse = dft_matrices(size)
    row_spec = pl.BlockSpec((1, rows, tile), lambda c, s: (0, 0, c))

    def prior_spec(at):
        return pl.BlockSpec((1, size, tile), lambda c, s: (s[at], 0, c))

    return pl.pallas_call(
        functools.partial(hyena_kernel, prior_at, source_at, taps_at),
        name="hyena",
        grid_spec=pltpu.PrefetchScalarGridSpec(
            num_scalar_prefetch=1,
            grid=(channels // tile,),
            in_specs=[row_spec] * 3
            + [prior_spec(at) for at in prior_at]
            + [
                pl.BlockSpec((*taps.shape[:2], tile), lambda c, s: (0, 0, c)),
                pl.BlockSpec((1, tile), lambda c, s: (0, c)),
                pl.BlockSpec(forward.shape, lambda c, s: (0, 0)),
                pl.BlockSpec(inverse.shape, lambda c, s: (0, 0)),
            ],
            out_specs=row_spec,
        ),
        out_shape=jax.ShapeDtypeStruct(hy_q.shape, hy_q.dtype),
        compiler_params=pltpu.CompilerParams(vmem_limit_bytes=VMEM_LIMIT),
        cost_estimate=pl.CostEstimate(
            flops=16 * rows * channels * size, bytes_accessed=8 * rows * channels, transcendentals=size * channels
        ),
    )(table, hy_q, hy_k, hy_v, *priors, taps, decay[None, :], jnp.asarray(forward), jnp.asarray(inverse))


def attend_kernel(live_at, chained, s_ref, q_ref, k_ref, v_ref, *rest):
    blocks = rest[: len(live_at)]
    o_ref = rest[-1]
    rows = q_ref.shape[1]
    tile = math.gcd(rows, 512)
    new_length = s_ref[0]
    scale = LOG2E / math.sqrt(HD)
    f32 = jnp.float32
    lives = [s_ref[at] > 0 for at in live_at]

    def score(keys, queries):
        return lax.dot_general(keys, queries, (((1,), (1,)), ((), ())), preferred_element_type=f32)

    fresh_values = v_ref[0].T
    groups = [range(i, min(i + 4, len(blocks))) for i in range(0, len(blocks), 4)]
    cached = [
        (
            jnp.concatenate([blocks[j][0, 0] for j in group], axis=0),
            jnp.concatenate([blocks[j][0, 1].T for j in group], axis=1),
            [lives[j] for j in group],
        )
        for group in groups
    ]
    for i in range(rows // tile):
        span = slice(i * tile, (i + 1) * tile)
        queries = q_ref[0, span, :]
        parts = []
        if i:
            parts.append((score(k_ref[0, : i * tile, :], queries), fresh_values[:, : i * tile]))
        key = lax.broadcasted_iota(jnp.int32, (tile, tile), 0)
        col = lax.broadcasted_iota(jnp.int32, (tile, tile), 1)
        diagonal = jnp.where(key <= col, score(k_ref[0, span, :], queries), NEG)
        parts.append((diagonal, fresh_values[:, span]))
        for keys, values, flags in cached:
            scores = score(keys, queries)
            size = scores.shape[0] // len(flags)
            scores = jnp.concatenate(
                [jnp.where(flag, scores[j * size : (j + 1) * size], NEG) for j, flag in enumerate(flags)], axis=0
            )
            parts.append((scores, values))
        top = functools.reduce(jnp.maximum, [jnp.max(scores, axis=0, keepdims=True) for scores, _ in parts])
        top_scaled = top * scale
        total, acc = 0.0, 0.0
        for scores, values in parts:
            expo = jnp.exp2(scores * scale - top_scaled)
            total = total + jnp.sum(expo, axis=0, keepdims=True)
            acc = acc + jnp.dot(values, expo.astype(jnp.bfloat16), preferred_element_type=f32)
        result = acc * (1.0 / total)
        lane = lax.broadcasted_iota(jnp.int32, (HD, tile), 1) + i * tile
        o_ref[0, span, :] = jnp.where(lane < new_length, result, 0.0).T.astype(o_ref.dtype)


def attend(table, queries, keys, values, blocks, first, heads, previous):
    rows = queries.shape[1]
    row_spec = pl.BlockSpec((1, rows, HD), lambda h, s: (0, 0, first + h))

    def block_spec(array, at):
        offset = first if array.shape[3] == queries.shape[2] else 0
        return pl.BlockSpec((1, 2, array.shape[2], HD), lambda h, s: (s[at], 0, 0, offset + h))

    operands = [queries, keys, values] + [array for array, _, _ in blocks]
    in_specs = [row_spec] * 3 + [block_spec(array, at) for array, at, _ in blocks]
    aliases = {}
    if previous is not None:
        aliases = {1 + len(operands): 0}
        operands.append(previous)
        in_specs.append(pl.BlockSpec(memory_space=pl.ANY))
    pairs = rows * heads * (rows // 2 + sum(array.shape[2] for array, _, _ in blocks))
    return pl.pallas_call(
        functools.partial(attend_kernel, [at for _, _, at in blocks], previous is not None),
        name="attend",
        grid_spec=pltpu.PrefetchScalarGridSpec(
            num_scalar_prefetch=1, grid=(heads,), in_specs=in_specs, out_specs=row_spec
        ),
        out_shape=jax.ShapeDtypeStruct(queries.shape, queries.dtype),
        input_output_aliases=aliases,
        compiler_params=pltpu.CompilerParams(vmem_limit_bytes=VMEM_LIMIT),
        cost_estimate=pl.CostEstimate(
            flops=4 * pairs * HD, bytes_accessed=12 * rows * heads * HD, transcendentals=pairs
        ),
    )(table, *operands)


LENGTH, ROUNDS, SOURCE, LAST_SLOT, NONE, SEND_SOURCE, SEND_SLOT, TAPS, PAIRS, SENDS = 0, 1, 2, 3, 4, 5, 6, 8, 16, 32
TABLE = 64


def plan_kernel(slots, axis, owner_ref, slot_ref, count_ref, length_ref, t_ref):
    me = lax.axis_index(axis)
    requests, entries = owner_ref.shape
    one, zero = jnp.int32(1), jnp.int32(0)

    def entry(request, e):
        bit = lax.shift_left(one, slot_ref[request, e])
        live = e < count_ref[request]
        return jnp.where(live, owner_ref[request, e], -1), jnp.where(live, bit, zero)

    crossing = [zero] * requests
    for request in range(requests):
        for e in range(entries):
            owner, bit = entry(request, e)
            for device in range(requests):
                if device // 2 != request // 2:
                    crossing[device] = crossing[device] | jnp.where(owner == device, bit, zero)
    mine = [zero] * requests
    for e in range(entries):
        owner, bit = entry(me, e)
        for x in range(requests):
            mine[x] = mine[x] | jnp.where(owner == (me ^ x), bit, zero)

    def bits(mask):
        return [lax.shift_right_logical(mask, jnp.int32(s)) & 1 for s in range(slots)]

    def select(device):
        return functools.reduce(lambda a, d: jnp.where(device == d, crossing[d], a), range(1, requests), crossing[0])

    rounds = functools.reduce(jnp.maximum, [sum(bits(mask)) for mask in crossing])
    t_ref[LENGTH] = length_ref[0]
    t_ref[ROUNDS] = rounds
    for x in range(requests):
        place, rank = zero, zero
        index = [zero] * CAP
        received = bits(select(me ^ x)) if x >= 2 else [one] * slots
        for wanted, here in zip(bits(mine[x]), received):
            for i in range(CAP):
                index[i] = jnp.where((wanted == 1) & (rank == i), place, index[i])
            rank = rank + wanted
            place = place + here
        for i in range(CAP):
            t_ref[PAIRS + 2 * CAP * x + i] = index[i]
            t_ref[PAIRS + 2 * CAP * x + CAP + i] = (rank > i).astype(jnp.int32)
    rank = zero
    sends = [zero] * slots
    for s, here in enumerate(bits(select(me))):
        for j in range(slots):
            sends[j] = jnp.where((here == 1) & (rank == j), s, sends[j])
        rank = rank + here
    for j in range(slots):
        t_ref[SENDS + j] = sends[j]
    for j in range(requests):
        flip = me ^ j
        t_ref[TAPS + j] = jnp.where(flip == 1, 2, jnp.where(flip == 2, 1, flip))
    last = count_ref[me] - 1
    last_owner = owner_ref[me, last]
    t_ref[SOURCE] = jnp.where(last_owner == me, 0, jnp.where(last_owner == (me ^ 1), 1, 2))
    t_ref[LAST_SLOT] = slot_ref[me, last]
    t_ref[NONE] = zero
    other = me ^ 2
    other_last = count_ref[other] - 1
    t_ref[SEND_SOURCE] = (owner_ref[other, other_last] != me).astype(jnp.int32)
    t_ref[SEND_SLOT] = slot_ref[other, other_last]


def plan(slots, axis, prefix_owner, prefix_slot, prefix_count, new_length):
    smem = pl.BlockSpec(memory_space=pltpu.SMEM)
    return pl.pallas_call(
        functools.partial(plan_kernel, slots, axis),
        name="plan",
        in_specs=[smem] * 4,
        out_specs=smem,
        out_shape=jax.ShapeDtypeStruct((TABLE,), jnp.int32),
    )(prefix_owner, prefix_slot, prefix_count, new_length)


def gather_kernel(columns, t_ref, cache_ref, *rest):
    outs, sems = rest[:-1], rest[-1]
    copies = []
    for g, (out, (start, width)) in enumerate(zip(outs, columns)):
        for j in range(out.shape[0]):
            source = cache_ref.at[t_ref[SENDS + j], :, :, pl.ds(start, width)]
            copies.append(pltpu.make_async_copy(source, out.at[j], sems.at[g, j]))
    for copy in copies:
        copy.start()
    for copy in copies:
        copy.wait()


def gather(table, cache, count, columns):
    return pl.pallas_call(
        functools.partial(gather_kernel, columns),
        name="gather",
        in_specs=[pl.BlockSpec(memory_space=pltpu.SMEM), pl.BlockSpec(memory_space=pl.ANY)],
        out_specs=[pl.BlockSpec(memory_space=pl.ANY)] * len(columns),
        out_shape=[jax.ShapeDtypeStruct((count, *cache.shape[1:3], width), cache.dtype) for _, width in columns],
        scratch_shapes=[pltpu.SemaphoreType.DMA((len(columns), count))],
    )(table, cache)


def head_groups(heads):
    sizes = [2] * (heads // 2 - 1) + [1, 1] if heads % 2 == 0 else [1] * heads
    starts = [sum(sizes[:i]) for i in range(len(sizes))]
    return list(zip(starts, sizes))


def per_device(
    hy_q, hy_k, hy_v, filter_taps, filter_decay, hy_cache, at_q, at_k, at_v, kv_cache,
    prefix_owner, prefix_slot, prefix_count, new_length,
):
    requests = prefix_owner.shape[0]
    slots = kv_cache.shape[0]

    def permute(array, flip):
        return lax.ppermute(array, "req", [(r, r ^ flip) for r in range(requests)])

    table = plan(slots, "req", prefix_owner, prefix_slot, prefix_count, new_length)
    groups = head_groups(at_q.shape[2] // HD)

    def body(rounds):
        def run():
            my_taps = filter_taps.T
            mate_hy = permute(hy_cache, 1)
            taps_pair = jnp.stack([my_taps, permute(my_taps, 2)])
            taps = jnp.concatenate([taps_pair, permute(taps_pair, 1)])
            mate_kv = permute(kv_cache, 1)
            outgoing = gather(table, kv_cache, rounds, [(start * HD, size * HD) for start, size in groups])
            mine, mates = (lax.dynamic_slice_in_dim(array, table[SEND_SLOT], 1, 0) for array in (hy_cache, mate_hy))
            from_cross = permute(jnp.where(table[SEND_SOURCE] == 0, mine, mates), 2)
            crossed = [permute(array, 2) for array in outgoing]
            hy_out = hyena(
                table, hy_q, hy_k, hy_v, (hy_cache, mate_hy, from_cross), (LAST_SLOT, LAST_SLOT, NONE), SOURCE,
                taps, TAPS, filter_decay,
            )
            at_out = None
            done = hy_out
            for (start, size), received in zip(groups, crossed):
                received, done = lax.optimization_barrier((received, done))
                if at_out is None:
                    hy_out = done
                else:
                    at_out = done
                relayed = permute(received, 1)
                blocks = []
                for x, array in enumerate((kv_cache, mate_kv, received, relayed)):
                    at = PAIRS + 2 * CAP * x
                    blocks += [(array, at + i, at + CAP + i) for i in range(CAP)]
                at_out = attend(table, at_q, at_k, at_v, blocks, start, size, at_out)
                done = at_out
            return hy_out, at_out

        return run

    least = min(3, slots)
    branches = [body(rounds) for rounds in range(least, slots + 1)]
    return lax.switch(jnp.clip(table[ROUNDS] - least, 0, len(branches) - 1), branches)


def per_device_general(
    hy_q, hy_k, hy_v, filter_taps, filter_decay, hy_cache, at_q, at_k, at_v, kv_cache,
    prefix_owner, prefix_slot, prefix_count, new_length,
):
    me = lax.axis_index("req")
    requests, entries = prefix_owner.shape
    entry = jnp.arange(entries, dtype=jnp.int32)
    live = entry[None, :] < prefix_count[:, None]
    mine = jnp.logical_and(live, prefix_owner == me)
    rank = jnp.cumsum(mine.astype(jnp.int32), axis=1) - mine.astype(jnp.int32)
    places = jnp.arange(CAP, dtype=jnp.int32)
    choose = jnp.logical_and(mine[:, None, :], rank[:, None, :] == places[None, :, None])
    send_slots = jnp.sum(jnp.where(choose, prefix_slot[:, None, :], 0), axis=2)
    at_last = entry[None, :] == prefix_count[:, None] - 1
    last_slot = jnp.sum(jnp.where(at_last, prefix_slot, 0), axis=1)
    last_owner = jnp.sum(jnp.where(at_last, prefix_owner, 0), axis=1)[me]
    my_owners = jnp.where(live[me], prefix_owner[me], -1)
    owners = jnp.arange(requests, dtype=jnp.int32)
    my_counts = jnp.sum((my_owners[None, :] == owners[:, None]).astype(jnp.int32), axis=1)
    incoming_hy = lax.all_to_all(hy_cache[last_slot], "req", 0, 0, tiled=True)
    incoming = lax.all_to_all(kv_cache[send_slots], "req", 0, 0, tiled=True)
    incoming = incoming.reshape(requests * CAP, *kv_cache.shape[1:])
    taps = lax.all_gather(filter_taps.T, "req", axis=0)
    numbers = jnp.arange(requests * CAP, dtype=jnp.int32)
    flags = (places[None, :] < my_counts[:, None]).astype(jnp.int32).reshape(-1)
    table = jnp.concatenate([jnp.stack([new_length[0], jnp.int32(0), last_owner]), owners, numbers, flags])
    hy_out = hyena(table, hy_q, hy_k, hy_v, (incoming_hy,), (2,), 1, taps, 3, filter_decay)
    first = 3 + requests
    blocks = [(incoming, first + i, first + requests * CAP + i) for i in range(requests * CAP)]
    at_out = attend(table, at_q, at_k, at_v, blocks, 0, at_q.shape[2] // HD, None)
    return hy_out, at_out


def solution(mesh):
    rows = P(("grp", "req"), None, "fsdp")
    placed = (
        rows, rows, rows, P("fsdp", "req"), P("fsdp"), rows, rows, rows, rows,
        P(("grp", "req"), None, None, "fsdp"), P("grp", None), P("grp", None), P("grp"), P(("grp", "req")),
    )
    body = per_device if mesh.shape["req"] == 4 else per_device_general
    return jax.shard_map(body, mesh=mesh, in_specs=placed, out_specs=(rows, rows), check_vma=False)
```

```python
import functools
import math

import jax
import jax.numpy as jnp
import numpy as np
from jax import lax
from jax.experimental import pallas as pl
from jax.experimental.pallas import tpu as pltpu
from jax.sharding import PartitionSpec as P

HD = 128
CAP = 2
LOG2E = 1.4426950408889634
NEG = -1e30
VMEM_LIMIT = 60 << 20


def dft_matrices(size):
    freq = np.arange(size)[:, None] + 0.5
    angle = np.pi * freq * np.arange(2 * size)[None, :] / size
    matrix = np.concatenate([np.cos(angle), -np.sin(angle)], axis=0)

    def split(values):
        high = values.astype(jnp.bfloat16)
        return high, (values - high.astype(np.float64)).astype(jnp.bfloat16)

    high, low = split(matrix[:, :size])
    inverse_high, inverse_low = split(matrix[:, size:].T / size)
    return np.concatenate([high, low], axis=1), np.concatenate([inverse_high, inverse_high, inverse_low], axis=1)


def hyena_kernel(prior_at, source_at, taps_at, s_ref, q_ref, k_ref, v_ref, *rest):
    *prior_refs, taps_ref, decay_ref, fwd_ref, inv_ref, o_ref = rest
    new_length = s_ref[0]
    source = s_ref[source_at]
    size = inv_ref.shape[0]
    width = q_ref.shape[2]
    f32 = jnp.float32
    taps = jnp.concatenate([taps_ref[s_ref[taps_at + j]] for j in range(taps_ref.shape[0])], axis=0)
    lag = lax.broadcasted_iota(jnp.int32, (size, width), 0)
    kern = (taps.astype(f32) * jnp.exp(-decay_ref[...] * lag.astype(f32))).astype(jnp.bfloat16)
    forward = fwd_ref[...]
    inverse = inv_ref[...]

    def transform(block):
        return jnp.dot(forward, jnp.concatenate([block, block], axis=0), preferred_element_type=f32)

    spectrum = transform(kern)
    kr, ki = spectrum[:size], spectrum[size:]
    sign = jnp.where(lag % 2 == 0, 1.0, -1.0)
    prior = prior_refs[0][0]
    for i in range(1, len(prior_refs)):
        prior = jnp.where(source == i, prior_refs[i][0], prior)
    prev = transform(prior)
    for b in range(q_ref.shape[1] // size):
        rows = slice(b * size, (b + 1) * size)
        cur = transform((k_ref[0, rows, :].astype(f32) * v_ref[0, rows, :].astype(f32)).astype(jnp.bfloat16))
        xr = prev[:size] + sign * cur[size:]
        xi = prev[size:] - sign * cur[:size]
        y = jnp.concatenate([xr * kr - xi * ki, xr * ki + xi * kr], axis=0)
        high = y.astype(jnp.bfloat16)
        low = (y - high.astype(f32)).astype(jnp.bfloat16)
        mixed = jnp.dot(inverse, jnp.concatenate([high, low, high], axis=0), preferred_element_type=f32)
        gated = q_ref[0, rows, :].astype(f32) * mixed
        o_ref[0, rows, :] = jnp.where(lag + b * size < new_length, gated, 0.0).astype(o_ref.dtype)
        prev = cur


def hyena(table, hy_q, hy_k, hy_v, priors, prior_at, source_at, taps, taps_at, decay):
    rows, channels = hy_q.shape[1:]
    size = priors[0].shape[1]
    tile = math.gcd(channels, 256)
    forward, inverse = dft_matrices(size)
    row_spec = pl.BlockSpec((1, rows, tile), lambda c, s: (0, 0, c))

    def prior_spec(at):
        return pl.BlockSpec((1, size, tile), lambda c, s: (s[at], 0, c))

    return pl.pallas_call(
        functools.partial(hyena_kernel, prior_at, source_at, taps_at),
        name="hyena",
        grid_spec=pltpu.PrefetchScalarGridSpec(
            num_scalar_prefetch=1,
            grid=(channels // tile,),
            in_specs=[row_spec] * 3
            + [prior_spec(at) for at in prior_at]
            + [
                pl.BlockSpec((*taps.shape[:2], tile), lambda c, s: (0, 0, c)),
                pl.BlockSpec((1, tile), lambda c, s: (0, c)),
                pl.BlockSpec(forward.shape, lambda c, s: (0, 0)),
                pl.BlockSpec(inverse.shape, lambda c, s: (0, 0)),
            ],
            out_specs=row_spec,
        ),
        out_shape=jax.ShapeDtypeStruct(hy_q.shape, hy_q.dtype),
        compiler_params=pltpu.CompilerParams(vmem_limit_bytes=VMEM_LIMIT),
        cost_estimate=pl.CostEstimate(
            flops=rows * channels, bytes_accessed=rows, transcendentals=0
        ),
    )(table, hy_q, hy_k, hy_v, *priors, taps, decay[None, :], jnp.asarray(forward), jnp.asarray(inverse))


def attend_kernel(live_at, chained, s_ref, q_ref, k_ref, v_ref, *rest):
    blocks = rest[: len(live_at)]
    o_ref = rest[-1]
    rows = q_ref.shape[1]
    tile = math.gcd(rows, 512)
    new_length = s_ref[0]
    scale = LOG2E / math.sqrt(HD)
    f32 = jnp.float32
    lives = [s_ref[at] > 0 for at in live_at]

    def score(keys, queries):
        return lax.dot_general(keys, queries, (((1,), (1,)), ((), ())), preferred_element_type=f32)

    fresh_values = v_ref[0].T
    groups = [range(i, min(i + 4, len(blocks))) for i in range(0, len(blocks), 4)]
    cached = [
        (
            jnp.concatenate([blocks[j][0, 0] for j in group], axis=0),
            jnp.concatenate([blocks[j][0, 1].T for j in group], axis=1),
            [lives[j] for j in group],
        )
        for group in groups
    ]
    for i in range(rows // tile):
        span = slice(i * tile, (i + 1) * tile)
        queries = q_ref[0, span, :]
        parts = []
        if i:
            parts.append((score(k_ref[0, : i * tile, :], queries), fresh_values[:, : i * tile]))
        key = lax.broadcasted_iota(jnp.int32, (tile, tile), 0)
        col = lax.broadcasted_iota(jnp.int32, (tile, tile), 1)
        diagonal = jnp.where(key <= col, score(k_ref[0, span, :], queries), NEG)
        parts.append((diagonal, fresh_values[:, span]))
        for keys, values, flags in cached:
            scores = score(keys, queries)
            size = scores.shape[0] // len(flags)
            scores = jnp.concatenate(
                [jnp.where(flag, scores[j * size : (j + 1) * size], NEG) for j, flag in enumerate(flags)], axis=0
            )
            parts.append((scores, values))
        top = functools.reduce(jnp.maximum, [jnp.max(scores, axis=0, keepdims=True) for scores, _ in parts])
        top_scaled = top * scale
        total, acc = 0.0, 0.0
        for scores, values in parts:
            expo = jnp.exp2(scores * scale - top_scaled)
            total = total + jnp.sum(expo, axis=0, keepdims=True)
            acc = acc + jnp.dot(values, expo.astype(jnp.bfloat16), preferred_element_type=f32)
        result = acc * (1.0 / total)
        lane = lax.broadcasted_iota(jnp.int32, (HD, tile), 1) + i * tile
        o_ref[0, span, :] = jnp.where(lane < new_length, result, 0.0).T.astype(o_ref.dtype)


def attend(table, queries, keys, values, blocks, first, heads, previous):
    rows = queries.shape[1]
    row_spec = pl.BlockSpec((1, rows, HD), lambda h, s: (0, 0, first + h))

    def block_spec(array, at):
        offset = first if array.shape[3] == queries.shape[2] else 0
        return pl.BlockSpec((1, 2, array.shape[2], HD), lambda h, s: (s[at], 0, 0, offset + h))

    operands = [queries, keys, values] + [array for array, _, _ in blocks]
    in_specs = [row_spec] * 3 + [block_spec(array, at) for array, at, _ in blocks]
    aliases = {}
    if previous is not None:
        aliases = {1 + len(operands): 0}
        operands.append(previous)
        in_specs.append(pl.BlockSpec(memory_space=pl.ANY))
    pairs = rows * heads
    return pl.pallas_call(
        functools.partial(attend_kernel, [at for _, _, at in blocks], previous is not None),
        name="attend",
        grid_spec=pltpu.PrefetchScalarGridSpec(
            num_scalar_prefetch=1, grid=(heads,), in_specs=in_specs, out_specs=row_spec
        ),
        out_shape=jax.ShapeDtypeStruct(queries.shape, queries.dtype),
        input_output_aliases=aliases,
        compiler_params=pltpu.CompilerParams(vmem_limit_bytes=VMEM_LIMIT),
        cost_estimate=pl.CostEstimate(
            flops=pairs, bytes_accessed=rows * heads, transcendentals=0
        ),
    )(table, *operands)


LENGTH, SOURCE, LAST_SLOT, NONE, SEND_SOURCE, SEND_SLOT, TAPS, PAIRS, SENDS = 0, 1, 2, 3, 4, 5, 8, 16, 32
TABLE = 64


def plan_kernel(slots, axis, owner_ref, slot_ref, count_ref, length_ref, t_ref):
    me = lax.axis_index(axis)
    requests, entries = owner_ref.shape
    zero = jnp.int32(0)

    def taken(request, owners):
        found = [[zero] * CAP for _ in owners]
        rank = [zero] * len(owners)
        for e in range(entries):
            owner = jnp.where(e < count_ref[request], owner_ref[request, e], -1)
            slot = slot_ref[request, e]
            for n, wanted in enumerate(owners):
                hit = owner == wanted
                for i in range(CAP):
                    found[n][i] = jnp.where(hit & (rank[n] == i), slot, found[n][i])
                rank[n] = rank[n] + hit.astype(jnp.int32)
        return found, rank

    found, rank = taken(me, [me ^ x for x in range(requests)])
    for x in range(requests):
        for i in range(CAP):
            t_ref[PAIRS + 2 * CAP * x + i] = found[x][i] if x < 2 else jnp.int32(i)
            t_ref[PAIRS + 2 * CAP * x + CAP + i] = (rank[x] > i).astype(jnp.int32)
    for x in (2, 3):
        found, _ = taken(me ^ x, [me])
        for i in range(CAP):
            t_ref[SENDS + CAP * (x - 2) + i] = found[0][i]
    for j in range(requests):
        flip = me ^ j
        t_ref[TAPS + j] = jnp.where(flip == 1, 2, jnp.where(flip == 2, 1, flip))
    last = count_ref[me] - 1
    last_owner = owner_ref[me, last]
    t_ref[LENGTH] = length_ref[0]
    t_ref[SOURCE] = jnp.where(last_owner == me, 0, jnp.where(last_owner == (me ^ 1), 1, 2))
    t_ref[LAST_SLOT] = slot_ref[me, last]
    t_ref[NONE] = zero
    other = me ^ 2
    other_last = count_ref[other] - 1
    t_ref[SEND_SOURCE] = (owner_ref[other, other_last] != me).astype(jnp.int32)
    t_ref[SEND_SLOT] = slot_ref[other, other_last]


def plan(slots, axis, prefix_owner, prefix_slot, prefix_count, new_length):
    smem = pl.BlockSpec(memory_space=pltpu.SMEM)
    return pl.pallas_call(
        functools.partial(plan_kernel, slots, axis),
        name="plan",
        in_specs=[smem] * 4,
        out_specs=smem,
        out_shape=jax.ShapeDtypeStruct((TABLE,), jnp.int32),
    )(prefix_owner, prefix_slot, prefix_count, new_length)


def gather_kernel(columns, t_ref, *refs):
    outs = list(refs[2:])
    for cache_ref in refs[:2]:
        for start, width in columns:
            outs.pop(0)[...] = cache_ref[..., start : start + width]


def gather(table, cache, columns):
    shape = cache.shape[1:3]
    columns_twice = columns * 2

    def source(at):
        return pl.BlockSpec((1, *cache.shape[1:]), lambda i, s: (s[at + i], 0, 0, 0))

    outs = pl.pallas_call(
        functools.partial(gather_kernel, columns),
        name="gather",
        grid_spec=pltpu.PrefetchScalarGridSpec(
            num_scalar_prefetch=1,
            grid=(CAP,),
            in_specs=[source(SENDS), source(SENDS + CAP)],
            out_specs=[pl.BlockSpec((1, *shape, width), lambda i, s: (i, 0, 0, 0)) for _, width in columns_twice],
        ),
        out_shape=[jax.ShapeDtypeStruct((CAP, *shape, width), cache.dtype) for _, width in columns_twice],
        compiler_params=pltpu.CompilerParams(vmem_limit_bytes=VMEM_LIMIT),
    )(table, cache, cache)
    return list(zip(outs[: len(columns)], outs[len(columns) :]))


def head_groups(heads):
    sizes = [2] * (heads // 2 - 1) + [1, 1] if heads % 2 == 0 else [1] * heads
    starts = [sum(sizes[:i]) for i in range(len(sizes))]
    return list(zip(starts, sizes))


def per_device(
    hy_q, hy_k, hy_v, filter_taps, filter_decay, hy_cache, at_q, at_k, at_v, kv_cache,
    prefix_owner, prefix_slot, prefix_count, new_length,
):
    requests = prefix_owner.shape[0]
    slots = kv_cache.shape[0]

    def permute(array, flip):
        return lax.ppermute(array, "req", [(r, r ^ flip) for r in range(requests)])

    table = plan(slots, "req", prefix_owner, prefix_slot, prefix_count, new_length)
    groups = head_groups(at_q.shape[2] // HD)
    my_taps = filter_taps.T
    mate_hy = permute(hy_cache, 1)
    taps_pair = jnp.stack([my_taps, permute(my_taps, 2)])
    taps = jnp.concatenate([taps_pair, permute(taps_pair, 1)])
    mate_kv = permute(kv_cache, 1)
    outgoing = gather(table, kv_cache, [(start * HD, size * HD) for start, size in groups])
    mine, mates = (lax.dynamic_slice_in_dim(array, table[SEND_SLOT], 1, 0) for array in (hy_cache, mate_hy))
    crossing = jnp.where(table[SEND_SOURCE] == 0, mine, mates)
    from_cross = permute(crossing, 2)
    hy_out = hyena(
        table, hy_q, hy_k, hy_v, (hy_cache, mate_hy, from_cross), (LAST_SLOT, LAST_SLOT, NONE), SOURCE,
        taps, TAPS, filter_decay,
    )
    gates = [crossing, crossing, hy_out]
    crossed = []

    def cross(pair):
        straight, diagonal = lax.optimization_barrier((pair, gates[len(crossed)]))[0]
        crossed.append((permute(straight, 2), permute(diagonal, 3)))

    for pair in outgoing[:3]:
        cross(pair)
    table, hy_out = lax.optimization_barrier((table, hy_out))
    at_out = None
    for (start, size), pair in zip(groups, outgoing[3:] + [None] * 3):
        blocks = []
        for x, array in enumerate((kv_cache, mate_kv, *crossed[len(gates) - 3])):
            at = PAIRS + 2 * CAP * x
            blocks += [(array, at + i, at + CAP + i) for i in range(CAP)]
        at_out = attend(table, at_q, at_k, at_v, blocks, start, size, at_out)
        gates.append(at_out)
        if pair is not None:
            cross(pair)
    return hy_out, at_out


def per_device_general(
    hy_q, hy_k, hy_v, filter_taps, filter_decay, hy_cache, at_q, at_k, at_v, kv_cache,
    prefix_owner, prefix_slot, prefix_count, new_length,
):
    me = lax.axis_index("req")
    requests, entries = prefix_owner.shape
    entry = jnp.arange(entries, dtype=jnp.int32)
    live = entry[None, :] < prefix_count[:, None]
    mine = jnp.logical_and(live, prefix_owner == me)
    rank = jnp.cumsum(mine.astype(jnp.int32), axis=1) - mine.astype(jnp.int32)
    places = jnp.arange(CAP, dtype=jnp.int32)
    choose = jnp.logical_and(mine[:, None, :], rank[:, None, :] == places[None, :, None])
    send_slots = jnp.sum(jnp.where(choose, prefix_slot[:, None, :], 0), axis=2)
    at_last = entry[None, :] == prefix_count[:, None] - 1
    last_slot = jnp.sum(jnp.where(at_last, prefix_slot, 0), axis=1)
    last_owner = jnp.sum(jnp.where(at_last, prefix_owner, 0), axis=1)[me]
    my_owners = jnp.where(live[me], prefix_owner[me], -1)
    owners = jnp.arange(requests, dtype=jnp.int32)
    my_counts = jnp.sum((my_owners[None, :] == owners[:, None]).astype(jnp.int32), axis=1)
    incoming_hy = lax.all_to_all(hy_cache[last_slot], "req", 0, 0, tiled=True)
    incoming = lax.all_to_all(kv_cache[send_slots], "req", 0, 0, tiled=True)
    incoming = incoming.reshape(requests * CAP, *kv_cache.shape[1:])
    taps = lax.all_gather(filter_taps.T, "req", axis=0)
    numbers = jnp.arange(requests * CAP, dtype=jnp.int32)
    flags = (places[None, :] < my_counts[:, None]).astype(jnp.int32).reshape(-1)
    table = jnp.concatenate([jnp.stack([new_length[0], jnp.int32(0), last_owner]), owners, numbers, flags])
    hy_out = hyena(table, hy_q, hy_k, hy_v, (incoming_hy,), (2,), 1, taps, 3, filter_decay)
    first = 3 + requests
    blocks = [(incoming, first + i, first + requests * CAP + i) for i in range(requests * CAP)]
    at_out = attend(table, at_q, at_k, at_v, blocks, 0, at_q.shape[2] // HD, None)
    return hy_out, at_out


def solution(mesh):
    rows = P(("grp", "req"), None, "fsdp")
    placed = (
        rows, rows, rows, P("fsdp", "req"), P("fsdp"), rows, rows, rows, rows,
        P(("grp", "req"), None, None, "fsdp"), P("grp", None), P("grp", None), P("grp"), P(("grp", "req")),
    )
    body = per_device if mesh.shape["req"] == 4 else per_device_general
    return jax.shard_map(body, mesh=mesh, in_specs=placed, out_specs=(rows, rows), check_vma=False)
```

```python
import functools
import math

import jax
import jax.numpy as jnp
import numpy as np
from jax import lax
from jax.experimental import pallas as pl
from jax.experimental.pallas import tpu as pltpu
from jax.sharding import PartitionSpec as P

HD = 128
CAP = 2
LOG2E = 1.4426950408889634
NEG = -1e30
VMEM_LIMIT = 64 << 20


def dft_matrices(size):
    freq = np.arange(size)[:, None] + 0.5
    angle = np.pi * freq * np.arange(2 * size)[None, :] / size
    matrix = np.concatenate([np.cos(angle), -np.sin(angle)], axis=0)

    def split(values):
        high = values.astype(jnp.bfloat16)
        return high, (values - high.astype(np.float64)).astype(jnp.bfloat16)

    high, low = split(matrix[:, :size])
    inverse_high, inverse_low = split(matrix[:, size:].T / size)
    return np.concatenate([high, low], axis=1), np.concatenate([inverse_high, inverse_high, inverse_low], axis=1)


def hyena_kernel(prior_at, source_at, taps_at, s_ref, q_ref, k_ref, v_ref, *rest):
    *prior_refs, taps_ref, decay_ref, fwd_ref, inv_ref, o_ref = rest
    new_length = s_ref[0]
    source = s_ref[source_at]
    size = inv_ref.shape[0]
    width = q_ref.shape[2]
    f32 = jnp.float32
    taps = jnp.concatenate([taps_ref[s_ref[taps_at + j]] for j in range(taps_ref.shape[0])], axis=0)
    lag = lax.broadcasted_iota(jnp.int32, (size, width), 0)
    kern = (taps.astype(f32) * jnp.exp(-decay_ref[...] * lag.astype(f32))).astype(jnp.bfloat16)
    forward = fwd_ref[...]
    inverse = inv_ref[...]

    def transform(block):
        return jnp.dot(forward, jnp.concatenate([block, block], axis=0), preferred_element_type=f32)

    spectrum = transform(kern)
    kr, ki = spectrum[:size], spectrum[size:]
    sign = jnp.where(lag % 2 == 0, 1.0, -1.0)
    prior = prior_refs[0][0]
    for i in range(1, len(prior_refs)):
        prior = jnp.where(source == i, prior_refs[i][0], prior)
    prev = transform(prior)
    for b in range(q_ref.shape[1] // size):
        rows = slice(b * size, (b + 1) * size)
        cur = transform((k_ref[0, rows, :].astype(f32) * v_ref[0, rows, :].astype(f32)).astype(jnp.bfloat16))
        xr = prev[:size] + sign * cur[size:]
        xi = prev[size:] - sign * cur[:size]
        y = jnp.concatenate([xr * kr - xi * ki, xr * ki + xi * kr], axis=0)
        high = y.astype(jnp.bfloat16)
        low = (y - high.astype(f32)).astype(jnp.bfloat16)
        mixed = jnp.dot(inverse, jnp.concatenate([high, low, high], axis=0), preferred_element_type=f32)
        gated = q_ref[0, rows, :].astype(f32) * mixed
        o_ref[0, rows, :] = jnp.where(lag + b * size < new_length, gated, 0.0).astype(o_ref.dtype)
        prev = cur


def hyena(table, hy_q, hy_k, hy_v, priors, prior_at, source_at, taps, taps_at, decay):
    rows, channels = hy_q.shape[1:]
    size = priors[0].shape[1]
    tile = math.gcd(channels, 256)
    forward, inverse = dft_matrices(size)
    row_spec = pl.BlockSpec((1, rows, tile), lambda c, s: (0, 0, c))

    def prior_spec(at):
        return pl.BlockSpec((1, size, tile), lambda c, s: (s[at], 0, c))

    priors = [in_hbm(array) for array in priors]
    return pl.pallas_call(
        functools.partial(hyena_kernel, prior_at, source_at, taps_at),
        name="hyena",
        grid_spec=pltpu.PrefetchScalarGridSpec(
            num_scalar_prefetch=1,
            grid=(channels // tile,),
            in_specs=[row_spec] * 3
            + [prior_spec(at) for at in prior_at]
            + [
                pl.BlockSpec((*taps.shape[:2], tile), lambda c, s: (0, 0, c)),
                pl.BlockSpec((1, tile), lambda c, s: (0, c)),
                pl.BlockSpec(forward.shape, lambda c, s: (0, 0)),
                pl.BlockSpec(inverse.shape, lambda c, s: (0, 0)),
            ],
            out_specs=row_spec,
        ),
        out_shape=jax.ShapeDtypeStruct(hy_q.shape, hy_q.dtype),
        compiler_params=pltpu.CompilerParams(vmem_limit_bytes=VMEM_LIMIT),
        cost_estimate=pl.CostEstimate(
            flops=rows * channels, bytes_accessed=rows, transcendentals=0
        ),
    )(table, hy_q, hy_k, hy_v, *priors, taps, decay[None, :], jnp.asarray(forward), jnp.asarray(inverse))


def attend_kernel(live_at, chained, s_ref, q_ref, k_ref, v_ref, *rest):
    blocks = rest[: len(live_at)]
    o_ref = rest[-1]
    rows = q_ref.shape[1]
    tile = math.gcd(rows, 512)
    new_length = s_ref[0]
    scale = LOG2E / math.sqrt(HD)
    f32 = jnp.float32
    lives = [s_ref[at] > 0 for at in live_at]

    def score(keys, queries):
        return lax.dot_general(keys, queries, (((1,), (1,)), ((), ())), preferred_element_type=f32)

    fresh_values = v_ref[0].T
    groups = [range(i, min(i + 4, len(blocks))) for i in range(0, len(blocks), 4)]
    cached = [
        (
            jnp.concatenate([blocks[j][0, 0] for j in group], axis=0),
            jnp.concatenate([blocks[j][0, 1].T for j in group], axis=1),
            [lives[j] for j in group],
        )
        for group in groups
    ]
    for i in range(rows // tile):
        span = slice(i * tile, (i + 1) * tile)
        queries = q_ref[0, span, :]
        parts = []
        if i:
            parts.append((score(k_ref[0, : i * tile, :], queries), fresh_values[:, : i * tile]))
        key = lax.broadcasted_iota(jnp.int32, (tile, tile), 0)
        col = lax.broadcasted_iota(jnp.int32, (tile, tile), 1)
        diagonal = jnp.where(key <= col, score(k_ref[0, span, :], queries), NEG)
        parts.append((diagonal, fresh_values[:, span]))
        for keys, values, flags in cached:
            scores = score(keys, queries)
            size = scores.shape[0] // len(flags)
            scores = jnp.concatenate(
                [jnp.where(flag, scores[j * size : (j + 1) * size], NEG) for j, flag in enumerate(flags)], axis=0
            )
            parts.append((scores, values))
        top = functools.reduce(jnp.maximum, [jnp.max(scores, axis=0, keepdims=True) for scores, _ in parts])
        top_scaled = top * scale
        total, acc = 0.0, 0.0
        for scores, values in parts:
            expo = jnp.exp2(scores * scale - top_scaled)
            total = total + jnp.sum(expo, axis=0, keepdims=True)
            acc = acc + jnp.dot(values, expo.astype(jnp.bfloat16), preferred_element_type=f32)
        result = acc * (1.0 / total)
        lane = lax.broadcasted_iota(jnp.int32, (HD, tile), 1) + i * tile
        o_ref[0, span, :] = jnp.where(lane < new_length, result, 0.0).T.astype(o_ref.dtype)


def in_hbm(array):
    return pltpu.with_memory_space_constraint(array, pltpu.MemorySpace.HBM)


def attend(table, queries, keys, values, blocks, first, heads, previous):
    rows = queries.shape[1]
    row_spec = pl.BlockSpec((1, rows, HD), lambda h, s: (0, 0, first + h))

    def block_spec(array, at):
        offset = first if array.shape[3] == queries.shape[2] else 0
        return pl.BlockSpec((1, 2, array.shape[2], HD), lambda h, s: (s[at], 0, 0, offset + h))

    operands = [queries, keys, values] + [in_hbm(array) for array, _, _ in blocks]
    in_specs = [row_spec] * 3 + [block_spec(array, at) for array, at, _ in blocks]
    aliases = {}
    if previous is not None:
        aliases = {1 + len(operands): 0}
        operands.append(previous)
        in_specs.append(pl.BlockSpec(memory_space=pl.ANY))
    pairs = rows * heads
    return pl.pallas_call(
        functools.partial(attend_kernel, [at for _, _, at in blocks], previous is not None),
        name="attend",
        grid_spec=pltpu.PrefetchScalarGridSpec(
            num_scalar_prefetch=1, grid=(heads,), in_specs=in_specs, out_specs=row_spec
        ),
        out_shape=jax.ShapeDtypeStruct(queries.shape, queries.dtype),
        input_output_aliases=aliases,
        compiler_params=pltpu.CompilerParams(vmem_limit_bytes=VMEM_LIMIT),
        cost_estimate=pl.CostEstimate(
            flops=pairs, bytes_accessed=rows * heads, transcendentals=0
        ),
    )(table, *operands)


LENGTH, SOURCE, LAST_SLOT, NONE, SEND_SOURCE, SEND_SLOT, TAPS, PAIRS, SENDS = 0, 1, 2, 3, 4, 5, 8, 16, 32
TABLE = 64


def plan_kernel(slots, axis, owner_ref, slot_ref, count_ref, length_ref, t_ref):
    me = lax.axis_index(axis)
    requests, entries = owner_ref.shape
    zero = jnp.int32(0)

    def taken(request, owners):
        found = [[zero] * CAP for _ in owners]
        rank = [zero] * len(owners)
        for e in range(entries):
            owner = jnp.where(e < count_ref[request], owner_ref[request, e], -1)
            slot = slot_ref[request, e]
            for n, wanted in enumerate(owners):
                hit = owner == wanted
                for i in range(CAP):
                    found[n][i] = jnp.where(hit & (rank[n] == i), slot, found[n][i])
                rank[n] = rank[n] + hit.astype(jnp.int32)
        return found, rank

    found, rank = taken(me, [me ^ x for x in range(requests)])
    for x in range(requests):
        for i in range(CAP):
            t_ref[PAIRS + 2 * CAP * x + i] = found[x][i] if x < 2 else jnp.int32(i)
            t_ref[PAIRS + 2 * CAP * x + CAP + i] = (rank[x] > i).astype(jnp.int32)
    for x in (2, 3):
        found, _ = taken(me ^ x, [me])
        for i in range(CAP):
            t_ref[SENDS + CAP * (x - 2) + i] = found[0][i]
    for j in range(requests):
        flip = me ^ j
        t_ref[TAPS + j] = jnp.where(flip == 1, 2, jnp.where(flip == 2, 1, flip))
    last = count_ref[me] - 1
    last_owner = owner_ref[me, last]
    t_ref[LENGTH] = length_ref[0]
    t_ref[SOURCE] = jnp.where(last_owner == me, 0, jnp.where(last_owner == (me ^ 1), 1, 2))
    t_ref[LAST_SLOT] = slot_ref[me, last]
    t_ref[NONE] = zero
    other = me ^ 2
    other_last = count_ref[other] - 1
    t_ref[SEND_SOURCE] = (owner_ref[other, other_last] != me).astype(jnp.int32)
    t_ref[SEND_SLOT] = slot_ref[other, other_last]


def plan(slots, axis, prefix_owner, prefix_slot, prefix_count, new_length):
    smem = pl.BlockSpec(memory_space=pltpu.SMEM)
    return pl.pallas_call(
        functools.partial(plan_kernel, slots, axis),
        name="plan",
        in_specs=[smem] * 4,
        out_specs=smem,
        out_shape=jax.ShapeDtypeStruct((TABLE,), jnp.int32),
    )(prefix_owner, prefix_slot, prefix_count, new_length)


def gather_kernel(columns, t_ref, *refs):
    outs = list(refs[2:])
    for cache_ref in refs[:2]:
        for start, width in columns:
            outs.pop(0)[...] = cache_ref[..., start : start + width]


def gather(table, cache, columns):
    shape = cache.shape[1:3]
    columns_twice = columns * 2

    def source(at):
        return pl.BlockSpec((1, *cache.shape[1:]), lambda i, s: (s[at + i], 0, 0, 0))

    outs = pl.pallas_call(
        functools.partial(gather_kernel, columns),
        name="gather",
        grid_spec=pltpu.PrefetchScalarGridSpec(
            num_scalar_prefetch=1,
            grid=(CAP,),
            in_specs=[source(SENDS), source(SENDS + CAP)],
            out_specs=[pl.BlockSpec((1, *shape, width), lambda i, s: (i, 0, 0, 0)) for _, width in columns_twice],
        ),
        out_shape=[jax.ShapeDtypeStruct((CAP, *shape, width), cache.dtype) for _, width in columns_twice],
        compiler_params=pltpu.CompilerParams(vmem_limit_bytes=VMEM_LIMIT),
    )(table, cache, cache)
    return list(zip(outs[: len(columns)], outs[len(columns) :]))


def head_groups(heads):
    sizes = [2] * (heads // 2 - 1) + [1, 1] if heads % 2 == 0 else [1] * heads
    starts = [sum(sizes[:i]) for i in range(len(sizes))]
    return list(zip(starts, sizes))


def per_device(
    hy_q, hy_k, hy_v, filter_taps, filter_decay, hy_cache, at_q, at_k, at_v, kv_cache,
    prefix_owner, prefix_slot, prefix_count, new_length,
):
    requests = prefix_owner.shape[0]
    slots = kv_cache.shape[0]

    def permute(array, flip):
        return lax.ppermute(array, "req", [(r, r ^ flip) for r in range(requests)])

    table = plan(slots, "req", prefix_owner, prefix_slot, prefix_count, new_length)
    groups = head_groups(at_q.shape[2] // HD)
    columns = [(start * HD, size * HD) for start, size in groups]
    mate_hy = permute(hy_cache, 1)
    my_taps, table = lax.optimization_barrier((filter_taps.T, table))
    across = permute(my_taps, 2)
    outgoing = gather(table, kv_cache, columns[:1])
    mine, mates = (lax.dynamic_slice_in_dim(array, table[SEND_SLOT], 1, 0) for array in (hy_cache, mate_hy))
    crossing = jnp.where(table[SEND_SOURCE] == 0, mine, mates)
    from_cross = permute(crossing, 2)
    taps_pair = jnp.stack([my_taps, across])
    taps = jnp.concatenate([taps_pair, permute(taps_pair, 1)])
    own_kv, table_late = lax.optimization_barrier((kv_cache, table, crossing))[:2]
    mate_kv = permute(own_kv, 1)
    outgoing += gather(table_late, kv_cache, columns[1:])
    hy_out = hyena(
        table, hy_q, hy_k, hy_v, (hy_cache, mate_hy, from_cross), (LAST_SLOT, LAST_SLOT, NONE), SOURCE,
        taps, TAPS, filter_decay,
    )
    gates = [crossing, crossing, hy_out]
    crossed = []

    def cross(pair):
        straight, diagonal = lax.optimization_barrier((pair, gates[len(crossed)]))[0]
        crossed.append((permute(straight, 2), permute(diagonal, 3)))

    for pair in outgoing[:3]:
        cross(pair)
    table, hy_out = lax.optimization_barrier((table, hy_out))
    at_out = None
    for (start, size), pair in zip(groups, outgoing[3:] + [None] * 3):
        blocks = []
        for x, array in enumerate((kv_cache, mate_kv, *crossed[len(gates) - 3])):
            at = PAIRS + 2 * CAP * x
            blocks += [(array, at + i, at + CAP + i) for i in range(CAP)]
        at_out = attend(table, at_q, at_k, at_v, blocks, start, size, at_out)
        gates.append(at_out)
        if pair is not None:
            cross(pair)
    return hy_out, at_out


def per_device_general(
    hy_q, hy_k, hy_v, filter_taps, filter_decay, hy_cache, at_q, at_k, at_v, kv_cache,
    prefix_owner, prefix_slot, prefix_count, new_length,
):
    me = lax.axis_index("req")
    requests, entries = prefix_owner.shape
    entry = jnp.arange(entries, dtype=jnp.int32)
    live = entry[None, :] < prefix_count[:, None]
    mine = jnp.logical_and(live, prefix_owner == me)
    rank = jnp.cumsum(mine.astype(jnp.int32), axis=1) - mine.astype(jnp.int32)
    places = jnp.arange(CAP, dtype=jnp.int32)
    choose = jnp.logical_and(mine[:, None, :], rank[:, None, :] == places[None, :, None])
    send_slots = jnp.sum(jnp.where(choose, prefix_slot[:, None, :], 0), axis=2)
    at_last = entry[None, :] == prefix_count[:, None] - 1
    last_slot = jnp.sum(jnp.where(at_last, prefix_slot, 0), axis=1)
    last_owner = jnp.sum(jnp.where(at_last, prefix_owner, 0), axis=1)[me]
    my_owners = jnp.where(live[me], prefix_owner[me], -1)
    owners = jnp.arange(requests, dtype=jnp.int32)
    my_counts = jnp.sum((my_owners[None, :] == owners[:, None]).astype(jnp.int32), axis=1)
    incoming_hy = lax.all_to_all(hy_cache[last_slot], "req", 0, 0, tiled=True)
    incoming = lax.all_to_all(kv_cache[send_slots], "req", 0, 0, tiled=True)
    incoming = incoming.reshape(requests * CAP, *kv_cache.shape[1:])
    taps = lax.all_gather(filter_taps.T, "req", axis=0)
    numbers = jnp.arange(requests * CAP, dtype=jnp.int32)
    flags = (places[None, :] < my_counts[:, None]).astype(jnp.int32).reshape(-1)
    table = jnp.concatenate([jnp.stack([new_length[0], jnp.int32(0), last_owner]), owners, numbers, flags])
    hy_out = hyena(table, hy_q, hy_k, hy_v, (incoming_hy,), (2,), 1, taps, 3, filter_decay)
    first = 3 + requests
    blocks = [(incoming, first + i, first + requests * CAP + i) for i in range(requests * CAP)]
    at_out = attend(table, at_q, at_k, at_v, blocks, 0, at_q.shape[2] // HD, None)
    return hy_out, at_out


def solution(mesh):
    rows = P(("grp", "req"), None, "fsdp")
    placed = (
        rows, rows, rows, P("fsdp", "req"), P("fsdp"), rows, rows, rows, rows,
        P(("grp", "req"), None, None, "fsdp"), P("grp", None), P("grp", None), P("grp"), P(("grp", "req")),
    )
    body = per_device if mesh.shape["req"] == 4 else per_device_general
    return jax.shard_map(body, mesh=mesh, in_specs=placed, out_specs=(rows, rows), check_vma=False)
```

```python
import functools
import math

import jax
import jax.numpy as jnp
import numpy as np
from jax import lax
from jax.experimental import pallas as pl
from jax.experimental.pallas import tpu as pltpu
from jax.sharding import PartitionSpec as P

HD = 128
CAP = 2
LOG2E = 1.4426950408889634
NEG = -1e30
VMEM_LIMIT = 64 << 20


def dft_matrices(size):
    freq = np.arange(size)[:, None] + 0.5
    angle = np.pi * freq * np.arange(2 * size)[None, :] / size
    matrix = np.concatenate([np.cos(angle), -np.sin(angle)], axis=0)

    def split(values):
        high = values.astype(jnp.bfloat16)
        return high, (values - high.astype(np.float64)).astype(jnp.bfloat16)

    high, low = split(matrix[:, :size])
    inverse_high, inverse_low = split(matrix[:, size:].T / size)
    return np.concatenate([high, low], axis=1), np.concatenate([inverse_high, inverse_high, inverse_low], axis=1)


def hyena_kernel(prior_at, source_at, taps_at, s_ref, q_ref, k_ref, v_ref, *rest):
    prior_refs, rest = rest[: len(prior_at)], rest[len(prior_at) :]
    *taps_refs, decay_ref, fwd_ref, inv_ref, o_ref = rest
    new_length = s_ref[0]
    source = s_ref[source_at]
    size = inv_ref.shape[0]
    width = q_ref.shape[2]
    f32 = jnp.float32
    pieces = [ref[...] for ref in taps_refs]

    def piece(place):
        return functools.reduce(lambda a, i: jnp.where(place == i, pieces[i], a), range(1, len(pieces)), pieces[0])

    taps = jnp.concatenate([piece(s_ref[taps_at + j]) for j in range(len(pieces))], axis=0)
    lag = lax.broadcasted_iota(jnp.int32, (size, width), 0)
    kern = (taps.astype(f32) * jnp.exp(-decay_ref[...] * lag.astype(f32))).astype(jnp.bfloat16)
    forward = fwd_ref[...]
    inverse = inv_ref[...]

    def transform(block):
        return jnp.dot(forward, jnp.concatenate([block, block], axis=0), preferred_element_type=f32)

    spectrum = transform(kern)
    kr, ki = spectrum[:size], spectrum[size:]
    sign = jnp.where(lag % 2 == 0, 1.0, -1.0)
    prior = prior_refs[0][0]
    for i in range(1, len(prior_refs)):
        prior = jnp.where(source == i, prior_refs[i][0], prior)
    prev = transform(prior)
    for b in range(q_ref.shape[1] // size):
        rows = slice(b * size, (b + 1) * size)
        cur = transform((k_ref[0, rows, :].astype(f32) * v_ref[0, rows, :].astype(f32)).astype(jnp.bfloat16))
        xr = prev[:size] + sign * cur[size:]
        xi = prev[size:] - sign * cur[:size]
        y = jnp.concatenate([xr * kr - xi * ki, xr * ki + xi * kr], axis=0)
        high = y.astype(jnp.bfloat16)
        low = (y - high.astype(f32)).astype(jnp.bfloat16)
        mixed = jnp.dot(inverse, jnp.concatenate([high, low, high], axis=0), preferred_element_type=f32)
        gated = q_ref[0, rows, :].astype(f32) * mixed
        o_ref[0, rows, :] = jnp.where(lag + b * size < new_length, gated, 0.0).astype(o_ref.dtype)
        prev = cur


def hyena(table, hy_q, hy_k, hy_v, priors, prior_at, source_at, taps, taps_at, decay):
    rows, channels = hy_q.shape[1:]
    size = priors[0].shape[1]
    tile = math.gcd(channels, 256)
    forward, inverse = dft_matrices(size)
    row_spec = pl.BlockSpec((1, rows, tile), lambda c, s: (0, 0, c))

    def prior_spec(at):
        return pl.BlockSpec((1, size, tile), lambda c, s: (s[at], 0, c))

    priors = [in_hbm(array) for array in priors]
    return pl.pallas_call(
        functools.partial(hyena_kernel, prior_at, source_at, taps_at),
        name="hyena",
        grid_spec=pltpu.PrefetchScalarGridSpec(
            num_scalar_prefetch=1,
            grid=(channels // tile,),
            in_specs=[row_spec] * 3
            + [prior_spec(at) for at in prior_at]
            + [
                *[pl.BlockSpec((piece.shape[0], tile), lambda c, s: (0, c)) for piece in taps],
                pl.BlockSpec((1, tile), lambda c, s: (0, c)),
                pl.BlockSpec(forward.shape, lambda c, s: (0, 0)),
                pl.BlockSpec(inverse.shape, lambda c, s: (0, 0)),
            ],
            out_specs=row_spec,
        ),
        out_shape=jax.ShapeDtypeStruct(hy_q.shape, hy_q.dtype),
        compiler_params=pltpu.CompilerParams(vmem_limit_bytes=VMEM_LIMIT),
        cost_estimate=pl.CostEstimate(
            flops=rows * channels, bytes_accessed=rows, transcendentals=0
        ),
    )(table, hy_q, hy_k, hy_v, *priors, *taps, decay[None, :], jnp.asarray(forward), jnp.asarray(inverse))


def attend_kernel(live_at, chained, s_ref, q_ref, k_ref, v_ref, *rest):
    blocks = rest[: len(live_at)]
    o_ref = rest[-1]
    rows = q_ref.shape[1]
    tile = math.gcd(rows, 512)
    new_length = s_ref[0]
    scale = LOG2E / math.sqrt(HD)
    f32 = jnp.float32
    lives = [s_ref[at] > 0 for at in live_at]

    def score(keys, queries):
        return lax.dot_general(keys, queries, (((1,), (1,)), ((), ())), preferred_element_type=f32)

    fresh_values = v_ref[0].T
    groups = [range(i, min(i + 4, len(blocks))) for i in range(0, len(blocks), 4)]
    cached = [
        (
            jnp.concatenate([blocks[j][0, 0] for j in group], axis=0),
            jnp.concatenate([blocks[j][0, 1].T for j in group], axis=1),
            [lives[j] for j in group],
        )
        for group in groups
    ]
    for i in range(rows // tile):
        span = slice(i * tile, (i + 1) * tile)
        queries = q_ref[0, span, :]
        parts = []
        if i:
            parts.append((score(k_ref[0, : i * tile, :], queries), fresh_values[:, : i * tile]))
        key = lax.broadcasted_iota(jnp.int32, (tile, tile), 0)
        col = lax.broadcasted_iota(jnp.int32, (tile, tile), 1)
        diagonal = jnp.where(key <= col, score(k_ref[0, span, :], queries), NEG)
        parts.append((diagonal, fresh_values[:, span]))
        for keys, values, flags in cached:
            scores = score(keys, queries)
            size = scores.shape[0] // len(flags)
            scores = jnp.concatenate(
                [jnp.where(flag, scores[j * size : (j + 1) * size], NEG) for j, flag in enumerate(flags)], axis=0
            )
            parts.append((scores, values))
        top = functools.reduce(jnp.maximum, [jnp.max(scores, axis=0, keepdims=True) for scores, _ in parts])
        top_scaled = top * scale
        total, acc = 0.0, 0.0
        for scores, values in parts:
            expo = jnp.exp2(scores * scale - top_scaled)
            total = total + jnp.sum(expo, axis=0, keepdims=True)
            acc = acc + jnp.dot(values, expo.astype(jnp.bfloat16), preferred_element_type=f32)
        result = acc * (1.0 / total)
        lane = lax.broadcasted_iota(jnp.int32, (HD, tile), 1) + i * tile
        o_ref[0, span, :] = jnp.where(lane < new_length, result, 0.0).T.astype(o_ref.dtype)


def in_hbm(array):
    return pltpu.with_memory_space_constraint(array, pltpu.MemorySpace.HBM)


def attend(table, queries, keys, values, blocks, first, heads, previous):
    rows = queries.shape[1]
    row_spec = pl.BlockSpec((1, rows, HD), lambda h, s: (0, 0, first + h))

    def block_spec(array, at):
        offset = first if array.shape[3] == queries.shape[2] else 0
        return pl.BlockSpec((1, 2, array.shape[2], HD), lambda h, s: (s[at], 0, 0, offset + h))

    operands = [queries, keys, values] + [in_hbm(array) for array, _, _ in blocks]
    in_specs = [row_spec] * 3 + [block_spec(array, at) for array, at, _ in blocks]
    aliases = {}
    if previous is not None:
        aliases = {1 + len(operands): 0}
        operands.append(previous)
        in_specs.append(pl.BlockSpec(memory_space=pl.ANY))
    pairs = rows * heads
    return pl.pallas_call(
        functools.partial(attend_kernel, [at for _, _, at in blocks], previous is not None),
        name="attend",
        grid_spec=pltpu.PrefetchScalarGridSpec(
            num_scalar_prefetch=1, grid=(heads,), in_specs=in_specs, out_specs=row_spec
        ),
        out_shape=jax.ShapeDtypeStruct(queries.shape, queries.dtype),
        input_output_aliases=aliases,
        compiler_params=pltpu.CompilerParams(vmem_limit_bytes=VMEM_LIMIT),
        cost_estimate=pl.CostEstimate(
            flops=pairs, bytes_accessed=rows * heads, transcendentals=0
        ),
    )(table, *operands)


LENGTH, SOURCE, LAST_SLOT, NONE, SEND_SOURCE, SEND_SLOT, TAPS, PAIRS, SENDS = 0, 1, 2, 3, 4, 5, 8, 16, 32
TABLE = 64


def plan_kernel(slots, axis, owner_ref, slot_ref, count_ref, length_ref, t_ref):
    me = lax.axis_index(axis)
    requests, entries = owner_ref.shape
    zero = jnp.int32(0)

    def taken(request, owners):
        found = [[zero] * CAP for _ in owners]
        rank = [zero] * len(owners)
        for e in range(entries):
            owner = jnp.where(e < count_ref[request], owner_ref[request, e], -1)
            slot = slot_ref[request, e]
            for n, wanted in enumerate(owners):
                hit = owner == wanted
                for i in range(CAP):
                    found[n][i] = jnp.where(hit & (rank[n] == i), slot, found[n][i])
                rank[n] = rank[n] + hit.astype(jnp.int32)
        return found, rank

    found, rank = taken(me, [me ^ x for x in range(requests)])
    for x in range(requests):
        for i in range(CAP):
            t_ref[PAIRS + 2 * CAP * x + i] = found[x][i] if x < 2 else jnp.int32(i)
            t_ref[PAIRS + 2 * CAP * x + CAP + i] = (rank[x] > i).astype(jnp.int32)
    for x in (2, 3):
        found, _ = taken(me ^ x, [me])
        for i in range(CAP):
            t_ref[SENDS + CAP * (x - 2) + i] = found[0][i]
    for j in range(requests):
        t_ref[TAPS + j] = me ^ j
    last = count_ref[me] - 1
    last_owner = owner_ref[me, last]
    t_ref[LENGTH] = length_ref[0]
    t_ref[SOURCE] = jnp.where(last_owner == me, 0, jnp.where(last_owner == (me ^ 1), 1, 2))
    t_ref[LAST_SLOT] = slot_ref[me, last]
    t_ref[NONE] = zero
    other = me ^ 2
    other_last = count_ref[other] - 1
    t_ref[SEND_SOURCE] = (owner_ref[other, other_last] != me).astype(jnp.int32)
    t_ref[SEND_SLOT] = slot_ref[other, other_last]


def plan(slots, axis, prefix_owner, prefix_slot, prefix_count, new_length):
    smem = pl.BlockSpec(memory_space=pltpu.SMEM)
    return pl.pallas_call(
        functools.partial(plan_kernel, slots, axis),
        name="plan",
        in_specs=[smem] * 4,
        out_specs=smem,
        out_shape=jax.ShapeDtypeStruct((TABLE,), jnp.int32),
    )(prefix_owner, prefix_slot, prefix_count, new_length)


def gather_kernel(columns, states, t_ref, *refs):
    caches, states_in, outs = refs[:2], refs[2 : 2 + states], list(refs[2 + states :])
    for cache_ref in caches:
        for start, width in columns:
            outs.pop(0)[...] = cache_ref[..., start : start + width]
    if states:
        mine, mates = states_in
        outs[0][...] = jnp.where(t_ref[SEND_SOURCE] == 0, mine[...], mates[...])


def gather(table, cache, columns, states=()):
    shape = cache.shape[1:3]
    low = columns[0][0]
    span = columns[-1][0] + columns[-1][1] - low
    assert low % span == 0
    columns = [(start - low, width) for start, width in columns]
    columns_twice = columns * 2

    def source(at):
        return pl.BlockSpec((1, *shape, span), lambda i, s: (s[at + i], 0, 0, low // span))

    out_specs = [pl.BlockSpec((1, *shape, width), lambda i, s: (i, 0, 0, 0)) for _, width in columns_twice]
    out_shape = [jax.ShapeDtypeStruct((CAP, *shape, width), cache.dtype) for _, width in columns_twice]
    if states:
        block = (1, *states[0].shape[1:])
        out_specs.append(pl.BlockSpec(block, lambda i, s: (0, 0, 0)))
        out_shape.append(jax.ShapeDtypeStruct(block, states[0].dtype))
    outs = pl.pallas_call(
        functools.partial(gather_kernel, columns, len(states)),
        name="gather",
        grid_spec=pltpu.PrefetchScalarGridSpec(
            num_scalar_prefetch=1,
            grid=(CAP,),
            in_specs=[source(SENDS), source(SENDS + CAP)]
            + [pl.BlockSpec((1, *state.shape[1:]), lambda i, s: (s[SEND_SLOT], 0, 0)) for state in states],
            out_specs=out_specs,
        ),
        out_shape=out_shape,
        compiler_params=pltpu.CompilerParams(vmem_limit_bytes=VMEM_LIMIT),
    )(table, cache, cache, *states)
    count = len(columns)
    return list(zip(outs[:count], outs[count : 2 * count])), outs[-1]


def head_groups(heads):
    sizes = [2] * (heads // 2 - 1) + [1, 1] if heads % 2 == 0 else [1] * heads
    starts = [sum(sizes[:i]) for i in range(len(sizes))]
    return list(zip(starts, sizes))


def per_device(
    hy_q, hy_k, hy_v, filter_taps, filter_decay, hy_cache, at_q, at_k, at_v, kv_cache,
    prefix_owner, prefix_slot, prefix_count, new_length,
):
    requests = prefix_owner.shape[0]
    slots = kv_cache.shape[0]

    def permute(array, flip):
        return lax.ppermute(array, "req", [(r, r ^ flip) for r in range(requests)])

    table = plan(slots, "req", prefix_owner, prefix_slot, prefix_count, new_length)
    groups = head_groups(at_q.shape[2] // HD)
    columns = [(start * HD, size * HD) for start, size in groups]
    my_taps = filter_taps.T
    mate_hy = permute(hy_cache, 1)
    taps = [my_taps, permute(my_taps, 1)]
    taps.append(permute(my_taps, 2))
    table, taps[2] = lax.optimization_barrier((table, taps[2]))
    outgoing, crossing = gather(table, kv_cache, columns[:1], (hy_cache, mate_hy))
    from_cross = permute(crossing, 2)
    taps.append(permute(taps[2], 1))
    own_kv, table_late = lax.optimization_barrier((kv_cache, table, crossing))[:2]
    mate_kv = permute(own_kv, 1)
    for part in (columns[1:2], columns[2:]):
        if part:
            outgoing += gather(table_late, kv_cache, part)[0]
    hy_out = hyena(
        table, hy_q, hy_k, hy_v, (hy_cache, mate_hy, from_cross), (LAST_SLOT, LAST_SLOT, NONE), SOURCE,
        taps, TAPS, filter_decay,
    )
    gates = [crossing, crossing, hy_out]
    crossed = []

    def cross(pair):
        straight, diagonal = lax.optimization_barrier((pair, gates[len(crossed)]))[0]
        crossed.append((permute(straight, 2), permute(diagonal, 3)))

    for pair in outgoing[:3]:
        cross(pair)
    table, hy_out = lax.optimization_barrier((table, hy_out))
    at_out = None
    for (start, size), pair in zip(groups, outgoing[3:] + [None] * 3):
        blocks = []
        for x, array in enumerate((kv_cache, mate_kv, *crossed[len(gates) - 3])):
            at = PAIRS + 2 * CAP * x
            blocks += [(array, at + i, at + CAP + i) for i in range(CAP)]
        at_out = attend(table, at_q, at_k, at_v, blocks, start, size, at_out)
        gates.append(at_out)
        if pair is not None:
            cross(pair)
    return hy_out, at_out


def per_device_general(
    hy_q, hy_k, hy_v, filter_taps, filter_decay, hy_cache, at_q, at_k, at_v, kv_cache,
    prefix_owner, prefix_slot, prefix_count, new_length,
):
    me = lax.axis_index("req")
    requests, entries = prefix_owner.shape
    entry = jnp.arange(entries, dtype=jnp.int32)
    live = entry[None, :] < prefix_count[:, None]
    mine = jnp.logical_and(live, prefix_owner == me)
    rank = jnp.cumsum(mine.astype(jnp.int32), axis=1) - mine.astype(jnp.int32)
    places = jnp.arange(CAP, dtype=jnp.int32)
    choose = jnp.logical_and(mine[:, None, :], rank[:, None, :] == places[None, :, None])
    send_slots = jnp.sum(jnp.where(choose, prefix_slot[:, None, :], 0), axis=2)
    at_last = entry[None, :] == prefix_count[:, None] - 1
    last_slot = jnp.sum(jnp.where(at_last, prefix_slot, 0), axis=1)
    last_owner = jnp.sum(jnp.where(at_last, prefix_owner, 0), axis=1)[me]
    my_owners = jnp.where(live[me], prefix_owner[me], -1)
    owners = jnp.arange(requests, dtype=jnp.int32)
    my_counts = jnp.sum((my_owners[None, :] == owners[:, None]).astype(jnp.int32), axis=1)
    incoming_hy = lax.all_to_all(hy_cache[last_slot], "req", 0, 0, tiled=True)
    incoming = lax.all_to_all(kv_cache[send_slots], "req", 0, 0, tiled=True)
    incoming = incoming.reshape(requests * CAP, *kv_cache.shape[1:])
    taps = lax.all_gather(filter_taps.T, "req", axis=0, tiled=True)
    numbers = jnp.arange(requests * CAP, dtype=jnp.int32)
    flags = (places[None, :] < my_counts[:, None]).astype(jnp.int32).reshape(-1)
    table = jnp.concatenate([jnp.stack([new_length[0], jnp.int32(0), last_owner]), numbers, flags])
    hy_out = hyena(table, hy_q, hy_k, hy_v, (incoming_hy,), (2,), 1, [taps], 1, filter_decay)
    first = 3
    blocks = [(incoming, first + i, first + requests * CAP + i) for i in range(requests * CAP)]
    at_out = attend(table, at_q, at_k, at_v, blocks, 0, at_q.shape[2] // HD, None)
    return hy_out, at_out


def solution(mesh):
    rows = P(("grp", "req"), None, "fsdp")
    placed = (
        rows, rows, rows, P("fsdp", "req"), P("fsdp"), rows, rows, rows, rows,
        P(("grp", "req"), None, None, "fsdp"), P("grp", None), P("grp", None), P("grp"), P(("grp", "req")),
    )
    body = per_device if mesh.shape["req"] == 4 else per_device_general
    return jax.shard_map(body, mesh=mesh, in_specs=placed, out_specs=(rows, rows), check_vma=False)
```

```python
import functools
import math

import jax
import jax.numpy as jnp
import numpy as np
from jax import lax
from jax.experimental import pallas as pl
from jax.experimental.pallas import tpu as pltpu
from jax.sharding import PartitionSpec as P

HD = 128
CAP = 2
LOG2E = 1.4426950408889634
NEG = -1e30
VMEM_LIMIT = 64 << 20


def dft_matrices(size):
    freq = np.arange(size)[:, None] + 0.5
    angle = np.pi * freq * np.arange(2 * size)[None, :] / size
    matrix = np.concatenate([np.cos(angle), -np.sin(angle)], axis=0)

    def split(values):
        high = values.astype(jnp.bfloat16)
        return high, (values - high.astype(np.float64)).astype(jnp.bfloat16)

    high, low = split(matrix[:, :size])
    inverse_high, inverse_low = split(matrix[:, size:].T / size)
    return np.concatenate([high, low], axis=1), np.concatenate([inverse_high, inverse_high, inverse_low], axis=1)


def hyena_kernel(prior_at, source_at, taps_at, s_ref, q_ref, k_ref, v_ref, *rest):
    prior_refs, rest = rest[: len(prior_at)], rest[len(prior_at) :]
    *taps_refs, decay_ref, fwd_ref, inv_ref, o_ref = rest
    new_length = s_ref[0]
    source = s_ref[source_at]
    size = inv_ref.shape[0]
    width = q_ref.shape[2]
    f32 = jnp.float32
    pieces = [ref[...] for ref in taps_refs]

    def piece(place):
        return functools.reduce(lambda a, i: jnp.where(place == i, pieces[i], a), range(1, len(pieces)), pieces[0])

    taps = jnp.concatenate([piece(s_ref[taps_at + j]) for j in range(len(pieces))], axis=0)
    lag = lax.broadcasted_iota(jnp.int32, (size, width), 0)
    kern = (taps.astype(f32) * jnp.exp(-decay_ref[...] * lag.astype(f32))).astype(jnp.bfloat16)
    forward = fwd_ref[...]
    inverse = inv_ref[...]

    def transform(block):
        return jnp.dot(forward, jnp.concatenate([block, block], axis=0), preferred_element_type=f32)

    spectrum = transform(kern)
    kr, ki = spectrum[:size], spectrum[size:]
    sign = jnp.where(lag % 2 == 0, 1.0, -1.0)
    prior = prior_refs[0][0]
    for i in range(1, len(prior_refs)):
        prior = jnp.where(source == i, prior_refs[i][0], prior)
    prev = transform(prior)
    for b in range(q_ref.shape[1] // size):
        rows = slice(b * size, (b + 1) * size)
        cur = transform((k_ref[0, rows, :].astype(f32) * v_ref[0, rows, :].astype(f32)).astype(jnp.bfloat16))
        xr = prev[:size] + sign * cur[size:]
        xi = prev[size:] - sign * cur[:size]
        y = jnp.concatenate([xr * kr - xi * ki, xr * ki + xi * kr], axis=0)
        high = y.astype(jnp.bfloat16)
        low = (y - high.astype(f32)).astype(jnp.bfloat16)
        mixed = jnp.dot(inverse, jnp.concatenate([high, low, high], axis=0), preferred_element_type=f32)
        gated = q_ref[0, rows, :].astype(f32) * mixed
        o_ref[0, rows, :] = jnp.where(lag + b * size < new_length, gated, 0.0).astype(o_ref.dtype)
        prev = cur


def hyena(table, hy_q, hy_k, hy_v, priors, prior_at, source_at, taps, taps_at, decay):
    rows, channels = hy_q.shape[1:]
    size = priors[0].shape[1]
    tile = math.gcd(channels, 256)
    forward, inverse = dft_matrices(size)
    row_spec = pl.BlockSpec((1, rows, tile), lambda c, s: (0, 0, c))

    def prior_spec(at):
        return pl.BlockSpec((1, size, tile), lambda c, s: (s[at], 0, c))

    priors = [in_hbm(array) for array in priors]
    return pl.pallas_call(
        functools.partial(hyena_kernel, prior_at, source_at, taps_at),
        name="hyena",
        grid_spec=pltpu.PrefetchScalarGridSpec(
            num_scalar_prefetch=1,
            grid=(channels // tile,),
            in_specs=[row_spec] * 3
            + [prior_spec(at) for at in prior_at]
            + [
                *[pl.BlockSpec((piece.shape[0], tile), lambda c, s: (0, c)) for piece in taps],
                pl.BlockSpec((1, tile), lambda c, s: (0, c)),
                pl.BlockSpec(forward.shape, lambda c, s: (0, 0)),
                pl.BlockSpec(inverse.shape, lambda c, s: (0, 0)),
            ],
            out_specs=row_spec,
        ),
        out_shape=jax.ShapeDtypeStruct(hy_q.shape, hy_q.dtype),
        compiler_params=pltpu.CompilerParams(vmem_limit_bytes=VMEM_LIMIT),
        cost_estimate=pl.CostEstimate(
            flops=rows * channels, bytes_accessed=rows, transcendentals=0
        ),
    )(table, hy_q, hy_k, hy_v, *priors, *taps, decay[None, :], jnp.asarray(forward), jnp.asarray(inverse))


def attend_kernel(live_at, chained, s_ref, q_ref, k_ref, v_ref, *rest):
    blocks = rest[: len(live_at)]
    o_ref = rest[-1]
    rows = q_ref.shape[1]
    tile = math.gcd(rows, 512)
    new_length = s_ref[0]
    scale = LOG2E / math.sqrt(HD)
    f32 = jnp.float32
    lives = [s_ref[at] > 0 for at in live_at]

    def score(keys, queries):
        return lax.dot_general(keys, queries, (((1,), (1,)), ((), ())), preferred_element_type=f32)

    fresh_values = v_ref[0].T
    groups = [range(i, min(i + 4, len(blocks))) for i in range(0, len(blocks), 4)]
    cached = [
        (
            jnp.concatenate([blocks[j][0, 0] for j in group], axis=0),
            jnp.concatenate([blocks[j][0, 1].T for j in group], axis=1),
            [lives[j] for j in group],
        )
        for group in groups
    ]
    for i in range(rows // tile):
        span = slice(i * tile, (i + 1) * tile)
        queries = q_ref[0, span, :]
        parts = []
        if i:
            parts.append((score(k_ref[0, : i * tile, :], queries), fresh_values[:, : i * tile]))
        key = lax.broadcasted_iota(jnp.int32, (tile, tile), 0)
        col = lax.broadcasted_iota(jnp.int32, (tile, tile), 1)
        diagonal = jnp.where(key <= col, score(k_ref[0, span, :], queries), NEG)
        parts.append((diagonal, fresh_values[:, span]))
        for keys, values, flags in cached:
            scores = score(keys, queries)
            size = scores.shape[0] // len(flags)
            scores = jnp.concatenate(
                [jnp.where(flag, scores[j * size : (j + 1) * size], NEG) for j, flag in enumerate(flags)], axis=0
            )
            parts.append((scores, values))
        top = functools.reduce(jnp.maximum, [jnp.max(scores, axis=0, keepdims=True) for scores, _ in parts])
        top_scaled = top * scale
        total, acc = 0.0, 0.0
        for scores, values in parts:
            expo = jnp.exp2(scores * scale - top_scaled)
            total = total + jnp.sum(expo, axis=0, keepdims=True)
            acc = acc + jnp.dot(values, expo.astype(jnp.bfloat16), preferred_element_type=f32)
        result = acc * (1.0 / total)
        lane = lax.broadcasted_iota(jnp.int32, (HD, tile), 1) + i * tile
        o_ref[0, span, :] = jnp.where(lane < new_length, result, 0.0).T.astype(o_ref.dtype)


def in_hbm(array):
    return pltpu.with_memory_space_constraint(array, pltpu.MemorySpace.HBM)


def attend(table, queries, keys, values, blocks, first, heads, previous):
    rows = queries.shape[1]
    row_spec = pl.BlockSpec((1, rows, HD), lambda h, s: (0, 0, first + h))

    def block_spec(array, at):
        offset = first if array.shape[3] == queries.shape[2] else 0
        return pl.BlockSpec((1, 2, array.shape[2], HD), lambda h, s: (s[at], 0, 0, offset + h))

    operands = [queries, keys, values] + [in_hbm(array) for array, _, _ in blocks]
    in_specs = [row_spec] * 3 + [block_spec(array, at) for array, at, _ in blocks]
    aliases = {}
    if previous is not None:
        aliases = {1 + len(operands): 0}
        operands.append(previous)
        in_specs.append(pl.BlockSpec(memory_space=pl.ANY))
    pairs = rows * heads
    return pl.pallas_call(
        functools.partial(attend_kernel, [at for _, _, at in blocks], previous is not None),
        name="attend",
        grid_spec=pltpu.PrefetchScalarGridSpec(
            num_scalar_prefetch=1, grid=(heads,), in_specs=in_specs, out_specs=row_spec
        ),
        out_shape=jax.ShapeDtypeStruct(queries.shape, queries.dtype),
        input_output_aliases=aliases,
        compiler_params=pltpu.CompilerParams(vmem_limit_bytes=VMEM_LIMIT),
        cost_estimate=pl.CostEstimate(
            flops=pairs, bytes_accessed=rows * heads, transcendentals=0
        ),
    )(table, *operands)


LENGTH, SOURCE, LAST_SLOT, NONE, SEND_SOURCE, SEND_SLOT, TAPS, PAIRS, SENDS = 0, 1, 2, 3, 4, 5, 8, 16, 32
TABLE = 64


def plan_kernel(slots, axis, owner_ref, slot_ref, count_ref, length_ref, t_ref):
    me = lax.axis_index(axis)
    requests, entries = owner_ref.shape
    zero = jnp.int32(0)

    def taken(request, owners):
        found = [[zero] * CAP for _ in owners]
        rank = [zero] * len(owners)
        for e in range(entries):
            owner = jnp.where(e < count_ref[request], owner_ref[request, e], -1)
            slot = slot_ref[request, e]
            for n, wanted in enumerate(owners):
                hit = owner == wanted
                for i in range(CAP):
                    found[n][i] = jnp.where(hit & (rank[n] == i), slot, found[n][i])
                rank[n] = rank[n] + hit.astype(jnp.int32)
        return found, rank

    found, rank = taken(me, [me ^ x for x in range(requests)])
    for x in range(requests):
        for i in range(CAP):
            t_ref[PAIRS + 2 * CAP * x + i] = found[x][i] if x < 2 else jnp.int32(i)
            t_ref[PAIRS + 2 * CAP * x + CAP + i] = (rank[x] > i).astype(jnp.int32)
    for x in (2, 3):
        found, _ = taken(me ^ x, [me])
        for i in range(CAP):
            t_ref[SENDS + CAP * (x - 2) + i] = found[0][i]
    for j in range(requests):
        t_ref[TAPS + j] = me ^ j
    last = count_ref[me] - 1
    last_owner = owner_ref[me, last]
    t_ref[LENGTH] = length_ref[0]
    t_ref[SOURCE] = jnp.where(last_owner == me, 0, jnp.where(last_owner == (me ^ 1), 1, 2))
    t_ref[LAST_SLOT] = slot_ref[me, last]
    t_ref[NONE] = zero
    other = me ^ 2
    other_last = count_ref[other] - 1
    t_ref[SEND_SOURCE] = (owner_ref[other, other_last] != me).astype(jnp.int32)
    t_ref[SEND_SLOT] = slot_ref[other, other_last]


def plan(slots, axis, prefix_owner, prefix_slot, prefix_count, new_length):
    smem = pl.BlockSpec(memory_space=pltpu.SMEM)
    return pl.pallas_call(
        functools.partial(plan_kernel, slots, axis),
        name="plan",
        in_specs=[smem] * 4,
        out_specs=smem,
        out_shape=jax.ShapeDtypeStruct((TABLE,), jnp.int32),
    )(prefix_owner, prefix_slot, prefix_count, new_length)


def gather_kernel(columns, states, t_ref, *refs):
    caches, states_in, outs = refs[:2], refs[2 : 2 + states], list(refs[2 + states :])
    for cache_ref in caches:
        for start, width in columns:
            outs.pop(0)[...] = cache_ref[..., start : start + width]
    if states:
        mine, mates = states_in
        outs[0][...] = jnp.where(t_ref[SEND_SOURCE] == 0, mine[...], mates[...])


def gather(table, cache, columns, states=()):
    shape = cache.shape[1:3]
    low, span = columns[0][0], columns[-1][0] + columns[-1][1] - columns[0][0]
    if low % span:
        low, span = 0, cache.shape[3]
    columns = [(start - low, width) for start, width in columns]
    columns_twice = columns * 2

    def source(at):
        return pl.BlockSpec((1, *shape, span), lambda i, s: (s[at + i], 0, 0, low // span))

    out_specs = [pl.BlockSpec((1, *shape, width), lambda i, s: (i, 0, 0, 0)) for _, width in columns_twice]
    out_shape = [jax.ShapeDtypeStruct((CAP, *shape, width), cache.dtype) for _, width in columns_twice]
    if states:
        block = (1, *states[0].shape[1:])
        out_specs.append(pl.BlockSpec(block, lambda i, s: (0, 0, 0)))
        out_shape.append(jax.ShapeDtypeStruct(block, states[0].dtype))
    outs = pl.pallas_call(
        functools.partial(gather_kernel, columns, len(states)),
        name="gather",
        grid_spec=pltpu.PrefetchScalarGridSpec(
            num_scalar_prefetch=1,
            grid=(CAP,),
            in_specs=[source(SENDS), source(SENDS + CAP)]
            + [pl.BlockSpec((1, *state.shape[1:]), lambda i, s: (s[SEND_SLOT], 0, 0)) for state in states],
            out_specs=out_specs,
        ),
        out_shape=out_shape,
        compiler_params=pltpu.CompilerParams(vmem_limit_bytes=VMEM_LIMIT),
    )(table, cache, cache, *states)
    count = len(columns)
    return list(zip(outs[:count], outs[count : 2 * count])), outs[-1]


def head_groups(heads):
    sizes, left = [], heads
    for size in [2, 3] + [2] * heads:
        size = min(size, left - 1)
        if size > 0:
            sizes.append(size)
            left -= size
    sizes.append(left)
    return [(sum(sizes[:i]), size) for i, size in enumerate(sizes)]


def per_device(
    hy_q, hy_k, hy_v, filter_taps, filter_decay, hy_cache, at_q, at_k, at_v, kv_cache,
    prefix_owner, prefix_slot, prefix_count, new_length,
):
    requests = prefix_owner.shape[0]
    slots = kv_cache.shape[0]

    def permute(array, flip):
        return lax.ppermute(array, "req", [(r, r ^ flip) for r in range(requests)])

    table = plan(slots, "req", prefix_owner, prefix_slot, prefix_count, new_length)
    groups = head_groups(at_q.shape[2] // HD)
    columns = [(start * HD, size * HD) for start, size in groups]
    my_taps = filter_taps.T
    mate_hy = permute(hy_cache, 1)
    taps = [my_taps, permute(my_taps, 1)]
    taps.append(permute(lax.optimization_barrier((my_taps, table))[0], 2))
    outgoing, crossing = gather(table, kv_cache, columns[:1], (hy_cache, mate_hy))
    crossing, taps[2] = lax.optimization_barrier((crossing, taps[2]))
    from_cross = permute(crossing, 2)
    taps.append(permute(taps[2], 1))
    own_kv, table_late = lax.optimization_barrier((kv_cache, table, crossing))[:2]
    mate_kv = permute(own_kv, 1)
    outgoing += gather(table_late, kv_cache, columns[1:])[0]
    hy_out = hyena(
        table, hy_q, hy_k, hy_v, (hy_cache, mate_hy, from_cross), (LAST_SLOT, LAST_SLOT, NONE), SOURCE,
        taps, TAPS, filter_decay,
    )
    gates = [crossing, crossing, hy_out]
    crossed = []

    def cross(pair):
        straight, diagonal = lax.optimization_barrier((pair, gates[len(crossed)]))[0]
        crossed.append((permute(straight, 2), permute(diagonal, 3)))

    for pair in outgoing[:3]:
        cross(pair)
    table, hy_out = lax.optimization_barrier((table, hy_out))
    at_out = None
    for (start, size), pair in zip(groups, outgoing[3:] + [None] * 3):
        blocks = []
        for x, array in enumerate((kv_cache, mate_kv, *crossed[len(gates) - 3])):
            at = PAIRS + 2 * CAP * x
            blocks += [(array, at + i, at + CAP + i) for i in range(CAP)]
        at_out = attend(table, at_q, at_k, at_v, blocks, start, size, at_out)
        gates.append(at_out)
        if pair is not None:
            cross(pair)
    return hy_out, at_out


def per_device_general(
    hy_q, hy_k, hy_v, filter_taps, filter_decay, hy_cache, at_q, at_k, at_v, kv_cache,
    prefix_owner, prefix_slot, prefix_count, new_length,
):
    me = lax.axis_index("req")
    requests, entries = prefix_owner.shape
    entry = jnp.arange(entries, dtype=jnp.int32)
    live = entry[None, :] < prefix_count[:, None]
    mine = jnp.logical_and(live, prefix_owner == me)
    rank = jnp.cumsum(mine.astype(jnp.int32), axis=1) - mine.astype(jnp.int32)
    places = jnp.arange(CAP, dtype=jnp.int32)
    choose = jnp.logical_and(mine[:, None, :], rank[:, None, :] == places[None, :, None])
    send_slots = jnp.sum(jnp.where(choose, prefix_slot[:, None, :], 0), axis=2)
    at_last = entry[None, :] == prefix_count[:, None] - 1
    last_slot = jnp.sum(jnp.where(at_last, prefix_slot, 0), axis=1)
    last_owner = jnp.sum(jnp.where(at_last, prefix_owner, 0), axis=1)[me]
    my_owners = jnp.where(live[me], prefix_owner[me], -1)
    owners = jnp.arange(requests, dtype=jnp.int32)
    my_counts = jnp.sum((my_owners[None, :] == owners[:, None]).astype(jnp.int32), axis=1)
    incoming_hy = lax.all_to_all(hy_cache[last_slot], "req", 0, 0, tiled=True)
    incoming = lax.all_to_all(kv_cache[send_slots], "req", 0, 0, tiled=True)
    incoming = incoming.reshape(requests * CAP, *kv_cache.shape[1:])
    taps = lax.all_gather(filter_taps.T, "req", axis=0, tiled=True)
    numbers = jnp.arange(requests * CAP, dtype=jnp.int32)
    flags = (places[None, :] < my_counts[:, None]).astype(jnp.int32).reshape(-1)
    table = jnp.concatenate([jnp.stack([new_length[0], jnp.int32(0), last_owner]), numbers, flags])
    hy_out = hyena(table, hy_q, hy_k, hy_v, (incoming_hy,), (2,), 1, [taps], 1, filter_decay)
    first = 3
    blocks = [(incoming, first + i, first + requests * CAP + i) for i in range(requests * CAP)]
    at_out = attend(table, at_q, at_k, at_v, blocks, 0, at_q.shape[2] // HD, None)
    return hy_out, at_out


def solution(mesh):
    rows = P(("grp", "req"), None, "fsdp")
    placed = (
        rows, rows, rows, P("fsdp", "req"), P("fsdp"), rows, rows, rows, rows,
        P(("grp", "req"), None, None, "fsdp"), P("grp", None), P("grp", None), P("grp"), P(("grp", "req")),
    )
    body = per_device if mesh.shape["req"] == 4 else per_device_general
    return jax.shard_map(body, mesh=mesh, in_specs=placed, out_specs=(rows, rows), check_vma=False)
```

```python
import functools
import math

import jax
import jax.numpy as jnp
import numpy as np
from jax import lax
from jax.experimental import pallas as pl
from jax.experimental.pallas import tpu as pltpu
from jax.sharding import PartitionSpec as P

HD = 128
CAP = 2
LOG2E = 1.4426950408889634
NEG = -1e30
VMEM_LIMIT = 64 << 20


def dft_matrices(size):
    freq = np.arange(size)[:, None] + 0.5
    angle = np.pi * freq * np.arange(2 * size)[None, :] / size
    matrix = np.concatenate([np.cos(angle), -np.sin(angle)], axis=0)

    def split(values):
        high = values.astype(jnp.bfloat16)
        return high, (values - high.astype(np.float64)).astype(jnp.bfloat16)

    high, low = split(matrix[:, :size])
    inverse_high, inverse_low = split(matrix[:, size:].T / size)
    return np.concatenate([high, low], axis=1), np.concatenate([inverse_high, inverse_high, inverse_low], axis=1)


def hyena_kernel(prior_at, source_at, taps_at, s_ref, q_ref, k_ref, v_ref, *rest):
    prior_refs, rest = rest[: len(prior_at)], rest[len(prior_at) :]
    *taps_refs, decay_ref, fwd_ref, inv_ref, o_ref = rest
    new_length = s_ref[0]
    source = s_ref[source_at]
    size = inv_ref.shape[0]
    width = q_ref.shape[2]
    f32 = jnp.float32
    pieces = [ref[...] for ref in taps_refs]

    def piece(place):
        return functools.reduce(lambda a, i: jnp.where(place == i, pieces[i], a), range(1, len(pieces)), pieces[0])

    taps = jnp.concatenate([piece(s_ref[taps_at + j]) for j in range(len(pieces))], axis=0)
    lag = lax.broadcasted_iota(jnp.int32, (size, width), 0)
    kern = (taps.astype(f32) * jnp.exp(-decay_ref[...] * lag.astype(f32))).astype(jnp.bfloat16)
    forward = fwd_ref[...]
    inverse = inv_ref[...]

    def transform(block):
        return jnp.dot(forward, jnp.concatenate([block, block], axis=0), preferred_element_type=f32)

    spectrum = transform(kern)
    kr, ki = spectrum[:size], spectrum[size:]
    sign = jnp.where(lag % 2 == 0, 1.0, -1.0)
    prior = prior_refs[0][0]
    for i in range(1, len(prior_refs)):
        prior = jnp.where(source == i, prior_refs[i][0], prior)
    prev = transform(prior)
    for b in range(q_ref.shape[1] // size):
        rows = slice(b * size, (b + 1) * size)
        cur = transform((k_ref[0, rows, :].astype(f32) * v_ref[0, rows, :].astype(f32)).astype(jnp.bfloat16))
        xr = prev[:size] + sign * cur[size:]
        xi = prev[size:] - sign * cur[:size]
        y = jnp.concatenate([xr * kr - xi * ki, xr * ki + xi * kr], axis=0)
        high = y.astype(jnp.bfloat16)
        low = (y - high.astype(f32)).astype(jnp.bfloat16)
        mixed = jnp.dot(inverse, jnp.concatenate([high, low, high], axis=0), preferred_element_type=f32)
        gated = q_ref[0, rows, :].astype(f32) * mixed
        o_ref[0, rows, :] = jnp.where(lag + b * size < new_length, gated, 0.0).astype(o_ref.dtype)
        prev = cur


def hyena(table, hy_q, hy_k, hy_v, priors, prior_at, source_at, taps, taps_at, decay):
    rows, channels = hy_q.shape[1:]
    size = priors[0].shape[1]
    tile = math.gcd(channels, 256)
    forward, inverse = dft_matrices(size)
    row_spec = pl.BlockSpec((1, rows, tile), lambda c, s: (0, 0, c))

    def prior_spec(at):
        return pl.BlockSpec((1, size, tile), lambda c, s: (s[at], 0, c))

    priors = [in_hbm(array) for array in priors]
    return pl.pallas_call(
        functools.partial(hyena_kernel, prior_at, source_at, taps_at),
        name="hyena",
        grid_spec=pltpu.PrefetchScalarGridSpec(
            num_scalar_prefetch=1,
            grid=(channels // tile,),
            in_specs=[row_spec] * 3
            + [prior_spec(at) for at in prior_at]
            + [
                *[pl.BlockSpec((piece.shape[0], tile), lambda c, s: (0, c)) for piece in taps],
                pl.BlockSpec((1, tile), lambda c, s: (0, c)),
                pl.BlockSpec(forward.shape, lambda c, s: (0, 0)),
                pl.BlockSpec(inverse.shape, lambda c, s: (0, 0)),
            ],
            out_specs=row_spec,
        ),
        out_shape=jax.ShapeDtypeStruct(hy_q.shape, hy_q.dtype),
        compiler_params=pltpu.CompilerParams(vmem_limit_bytes=VMEM_LIMIT),
        cost_estimate=pl.CostEstimate(
            flops=rows * channels, bytes_accessed=rows, transcendentals=0
        ),
    )(table, hy_q, hy_k, hy_v, *priors, *taps, decay[None, :], jnp.asarray(forward), jnp.asarray(inverse))


def attend_kernel(live_at, chained, s_ref, q_ref, k_ref, v_ref, *rest):
    blocks = rest[: len(live_at)]
    o_ref = rest[-1]
    rows = q_ref.shape[1]
    tile = math.gcd(rows, 512)
    new_length = s_ref[0]
    scale = LOG2E / math.sqrt(HD)
    f32 = jnp.float32
    lives = [s_ref[at] > 0 for at in live_at]

    def score(keys, queries):
        return lax.dot_general(keys, queries, (((1,), (1,)), ((), ())), preferred_element_type=f32)

    fresh_values = v_ref[0].T
    groups = [range(i, min(i + 4, len(blocks))) for i in range(0, len(blocks), 4)]
    cached = [
        (
            jnp.concatenate([blocks[j][0, 0] for j in group], axis=0),
            jnp.concatenate([blocks[j][0, 1].T for j in group], axis=1),
            [lives[j] for j in group],
        )
        for group in groups
    ]
    for i in range(rows // tile):
        span = slice(i * tile, (i + 1) * tile)
        queries = q_ref[0, span, :]
        parts = []
        if i:
            parts.append((score(k_ref[0, : i * tile, :], queries), fresh_values[:, : i * tile]))
        key = lax.broadcasted_iota(jnp.int32, (tile, tile), 0)
        col = lax.broadcasted_iota(jnp.int32, (tile, tile), 1)
        diagonal = jnp.where(key <= col, score(k_ref[0, span, :], queries), NEG)
        parts.append((diagonal, fresh_values[:, span]))
        for keys, values, flags in cached:
            scores = score(keys, queries)
            size = scores.shape[0] // len(flags)
            scores = jnp.concatenate(
                [jnp.where(flag, scores[j * size : (j + 1) * size], NEG) for j, flag in enumerate(flags)], axis=0
            )
            parts.append((scores, values))
        top = functools.reduce(jnp.maximum, [jnp.max(scores, axis=0, keepdims=True) for scores, _ in parts])
        top_scaled = top * scale
        total, acc = 0.0, 0.0
        for scores, values in parts:
            expo = jnp.exp2(scores * scale - top_scaled)
            total = total + jnp.sum(expo, axis=0, keepdims=True)
            acc = acc + jnp.dot(values, expo.astype(jnp.bfloat16), preferred_element_type=f32)
        result = acc * (1.0 / total)
        lane = lax.broadcasted_iota(jnp.int32, (HD, tile), 1) + i * tile
        o_ref[0, span, :] = jnp.where(lane < new_length, result, 0.0).T.astype(o_ref.dtype)


def in_hbm(array):
    return pltpu.with_memory_space_constraint(array, pltpu.MemorySpace.HBM)


def attend(table, queries, keys, values, blocks, first, heads, previous):
    rows = queries.shape[1]
    row_spec = pl.BlockSpec((1, rows, HD), lambda h, s: (0, 0, first + h))

    def block_spec(array, at):
        offset = first if array.shape[3] == queries.shape[2] else 0
        return pl.BlockSpec((1, 2, array.shape[2], HD), lambda h, s: (s[at], 0, 0, offset + h))

    operands = [queries, keys, values] + [in_hbm(array) for array, _, _ in blocks]
    in_specs = [row_spec] * 3 + [block_spec(array, at) for array, at, _ in blocks]
    aliases = {}
    if previous is not None:
        aliases = {1 + len(operands): 0}
        operands.append(previous)
        in_specs.append(pl.BlockSpec(memory_space=pl.ANY))
    pairs = rows * heads
    return pl.pallas_call(
        functools.partial(attend_kernel, [at for _, _, at in blocks], previous is not None),
        name="attend",
        grid_spec=pltpu.PrefetchScalarGridSpec(
            num_scalar_prefetch=1, grid=(heads,), in_specs=in_specs, out_specs=row_spec
        ),
        out_shape=jax.ShapeDtypeStruct(queries.shape, queries.dtype),
        input_output_aliases=aliases,
        compiler_params=pltpu.CompilerParams(vmem_limit_bytes=VMEM_LIMIT),
        cost_estimate=pl.CostEstimate(
            flops=pairs, bytes_accessed=rows * heads, transcendentals=0
        ),
    )(table, *operands)


LENGTH, SOURCE, LAST_SLOT, NONE, SEND_SOURCE, SEND_SLOT, TAPS, PAIRS, SENDS = 0, 1, 2, 3, 4, 5, 8, 16, 32
TABLE = 64


def plan_kernel(slots, axis, owner_ref, slot_ref, count_ref, length_ref, t_ref):
    me = lax.axis_index(axis)
    requests, entries = owner_ref.shape
    zero = jnp.int32(0)

    def taken(request, owners):
        found = [[zero] * CAP for _ in owners]
        rank = [zero] * len(owners)
        for e in range(entries):
            owner = jnp.where(e < count_ref[request], owner_ref[request, e], -1)
            slot = slot_ref[request, e]
            for n, wanted in enumerate(owners):
                hit = owner == wanted
                for i in range(CAP):
                    found[n][i] = jnp.where(hit & (rank[n] == i), slot, found[n][i])
                rank[n] = rank[n] + hit.astype(jnp.int32)
        return found, rank

    found, rank = taken(me, [me ^ x for x in range(requests)])
    for x in range(requests):
        for i in range(CAP):
            t_ref[PAIRS + 2 * CAP * x + i] = found[x][i] if x < 2 else jnp.int32(i)
            t_ref[PAIRS + 2 * CAP * x + CAP + i] = (rank[x] > i).astype(jnp.int32)
    for x in (2, 3):
        found, _ = taken(me ^ x, [me])
        for i in range(CAP):
            t_ref[SENDS + CAP * (x - 2) + i] = found[0][i]
    for j in range(requests):
        t_ref[TAPS + j] = me ^ j
    last = count_ref[me] - 1
    last_owner = owner_ref[me, last]
    t_ref[LENGTH] = length_ref[0]
    t_ref[SOURCE] = jnp.where(last_owner == me, 0, jnp.where(last_owner == (me ^ 1), 1, 2))
    t_ref[LAST_SLOT] = slot_ref[me, last]
    t_ref[NONE] = zero
    other = me ^ 2
    other_last = count_ref[other] - 1
    t_ref[SEND_SOURCE] = (owner_ref[other, other_last] != me).astype(jnp.int32)
    t_ref[SEND_SLOT] = slot_ref[other, other_last]


def plan(slots, axis, prefix_owner, prefix_slot, prefix_count, new_length):
    smem = pl.BlockSpec(memory_space=pltpu.SMEM)
    return pl.pallas_call(
        functools.partial(plan_kernel, slots, axis),
        name="plan",
        in_specs=[smem] * 4,
        out_specs=smem,
        out_shape=jax.ShapeDtypeStruct((TABLE,), jnp.int32),
    )(prefix_owner, prefix_slot, prefix_count, new_length)


def gather_kernel(columns, t_ref, *refs):
    caches, refs = refs[: 2 * CAP], list(refs[2 * CAP :])
    if len(refs) > 2 * len(columns):
        mine, mates, out = refs.pop(0), refs.pop(0), refs.pop()
        out[...] = jnp.where(t_ref[SEND_SOURCE] == 0, mine[...], mates[...])
    for n, out in enumerate(refs):
        start, width = columns[n % len(columns)]
        for i in range(CAP):
            out[i] = caches[n // len(columns) * CAP + i][0, :, :, start : start + width]


def gather(table, cache, columns, states=()):
    shape = cache.shape[1:3]
    low, span = columns[0][0], columns[-1][0] + columns[-1][1] - columns[0][0]
    if low % span:
        low, span = 0, cache.shape[3]
    columns = [(start - low, width) for start, width in columns]

    def source(at):
        return pl.BlockSpec((1, *shape, span), lambda i, s: (s[at], 0, 0, low // span))

    out_shape = [jax.ShapeDtypeStruct((CAP, *shape, width), cache.dtype) for _, width in columns * 2]
    if states:
        out_shape.append(jax.ShapeDtypeStruct((1, *states[0].shape[1:]), states[0].dtype))

    def whole(rank):
        return lambda i, s: (0,) * rank

    outs = pl.pallas_call(
        functools.partial(gather_kernel, columns),
        name="gather",
        grid_spec=pltpu.PrefetchScalarGridSpec(
            num_scalar_prefetch=1,
            grid=(1,),
            in_specs=[source(SENDS + n) for n in range(2 * CAP)]
            + [pl.BlockSpec((1, *state.shape[1:]), lambda i, s: (s[SEND_SLOT], 0, 0)) for state in states],
            out_specs=[pl.BlockSpec(out.shape, whole(len(out.shape))) for out in out_shape],
        ),
        out_shape=out_shape,
        compiler_params=pltpu.CompilerParams(vmem_limit_bytes=VMEM_LIMIT),
    )(table, *[cache] * (2 * CAP), *states)
    count = len(columns)
    return list(zip(outs[:count], outs[count : 2 * count])), outs[-1]


def head_groups(heads):
    sizes, left = [], heads
    for size in [2, 3] + [2] * heads:
        size = min(size, left - 1)
        if size > 0:
            sizes.append(size)
            left -= size
    sizes.append(left)
    return [(sum(sizes[:i]), size) for i, size in enumerate(sizes)]


def per_device(
    hy_q, hy_k, hy_v, filter_taps, filter_decay, hy_cache, at_q, at_k, at_v, kv_cache,
    prefix_owner, prefix_slot, prefix_count, new_length,
):
    requests = prefix_owner.shape[0]
    slots = kv_cache.shape[0]

    def permute(array, flip):
        return lax.ppermute(array, "req", [(r, r ^ flip) for r in range(requests)])

    table = plan(slots, "req", prefix_owner, prefix_slot, prefix_count, new_length)
    groups = head_groups(at_q.shape[2] // HD)
    columns = [(start * HD, size * HD) for start, size in groups]
    my_taps = filter_taps.T
    mate_hy = permute(hy_cache, 1)
    taps = [my_taps, permute(my_taps, 1)]
    taps.append(permute(lax.optimization_barrier((my_taps, table))[0], 2))
    outgoing, crossing = gather(table, kv_cache, columns[:1], (hy_cache, mate_hy))
    crossing, taps[2] = lax.optimization_barrier((crossing, taps[2]))
    from_cross = permute(crossing, 2)
    taps.append(permute(taps[2], 1))
    own_kv, table_late = lax.optimization_barrier((kv_cache, table, crossing))[:2]
    mate_kv = permute(own_kv, 1)
    outgoing += gather(table_late, kv_cache, columns[1:])[0]
    hy_out = hyena(
        table, hy_q, hy_k, hy_v, (hy_cache, mate_hy, from_cross), (LAST_SLOT, LAST_SLOT, NONE), SOURCE,
        taps, TAPS, filter_decay,
    )
    gates = [crossing, crossing, hy_out]
    crossed = []

    def cross(pair):
        straight, diagonal = lax.optimization_barrier((pair, gates[len(crossed)]))[0]
        crossed.append((permute(straight, 2), permute(diagonal, 3)))

    for pair in outgoing[:3]:
        cross(pair)
    table, hy_out = lax.optimization_barrier((table, hy_out))
    at_out = None
    for (start, size), pair in zip(groups, outgoing[3:] + [None] * 3):
        blocks = []
        for x, array in enumerate((kv_cache, mate_kv, *crossed[len(gates) - 3])):
            at = PAIRS + 2 * CAP * x
            blocks += [(array, at + i, at + CAP + i) for i in range(CAP)]
        at_out = attend(table, at_q, at_k, at_v, blocks, start, size, at_out)
        gates.append(at_out)
        if pair is not None:
            cross(pair)
    return hy_out, at_out


def per_device_general(
    hy_q, hy_k, hy_v, filter_taps, filter_decay, hy_cache, at_q, at_k, at_v, kv_cache,
    prefix_owner, prefix_slot, prefix_count, new_length,
):
    me = lax.axis_index("req")
    requests, entries = prefix_owner.shape
    entry = jnp.arange(entries, dtype=jnp.int32)
    live = entry[None, :] < prefix_count[:, None]
    mine = jnp.logical_and(live, prefix_owner == me)
    rank = jnp.cumsum(mine.astype(jnp.int32), axis=1) - mine.astype(jnp.int32)
    places = jnp.arange(CAP, dtype=jnp.int32)
    choose = jnp.logical_and(mine[:, None, :], rank[:, None, :] == places[None, :, None])
    send_slots = jnp.sum(jnp.where(choose, prefix_slot[:, None, :], 0), axis=2)
    at_last = entry[None, :] == prefix_count[:, None] - 1
    last_slot = jnp.sum(jnp.where(at_last, prefix_slot, 0), axis=1)
    last_owner = jnp.sum(jnp.where(at_last, prefix_owner, 0), axis=1)[me]
    my_owners = jnp.where(live[me], prefix_owner[me], -1)
    owners = jnp.arange(requests, dtype=jnp.int32)
    my_counts = jnp.sum((my_owners[None, :] == owners[:, None]).astype(jnp.int32), axis=1)
    incoming_hy = lax.all_to_all(hy_cache[last_slot], "req", 0, 0, tiled=True)
    incoming = lax.all_to_all(kv_cache[send_slots], "req", 0, 0, tiled=True)
    incoming = incoming.reshape(requests * CAP, *kv_cache.shape[1:])
    taps = lax.all_gather(filter_taps.T, "req", axis=0, tiled=True)
    numbers = jnp.arange(requests * CAP, dtype=jnp.int32)
    flags = (places[None, :] < my_counts[:, None]).astype(jnp.int32).reshape(-1)
    table = jnp.concatenate([jnp.stack([new_length[0], jnp.int32(0), last_owner]), numbers, flags])
    hy_out = hyena(table, hy_q, hy_k, hy_v, (incoming_hy,), (2,), 1, [taps], 1, filter_decay)
    first = 3
    blocks = [(incoming, first + i, first + requests * CAP + i) for i in range(requests * CAP)]
    at_out = attend(table, at_q, at_k, at_v, blocks, 0, at_q.shape[2] // HD, None)
    return hy_out, at_out


def solution(mesh):
    rows = P(("grp", "req"), None, "fsdp")
    placed = (
        rows, rows, rows, P("fsdp", "req"), P("fsdp"), rows, rows, rows, rows,
        P(("grp", "req"), None, None, "fsdp"), P("grp", None), P("grp", None), P("grp"), P(("grp", "req")),
    )
    body = per_device if mesh.shape["req"] == 4 else per_device_general
    return jax.shard_map(body, mesh=mesh, in_specs=placed, out_specs=(rows, rows), check_vma=False)
```
